128 devices in a mesh: pos: 4 (over x), depth: 32 (over z, y, core).
Axes of the slice: x: 4, y: 4, z: 4, core: 2. Of those that a mesh axis runs over, the one named last changes fastest.
Arguments:
- object_field: float32 [64, 2, 512, 512], P('depth', None, 'pos'), may hold values from -1.25 to 1.25, as said below
- offsets: int32 [8, 2], P('pos'), may hold values from 0 to 511, as said below
- probe: float32 [2, 128, 128], replicated, may hold values from -4.2 to 4.2
- intensity: float32 [8, 128, 128], P('pos'), may hold values from 0 to 2
Outputs:
- object_grad: float32 [64, 2, 512, 512], P('depth', None, 'pos')
The draws below stay inside these ranges and needn't reach their ends.
Inputs may be any that keep to these rules, and one draw needn't show every extreme that they name: `offsets`: the row of position p lies in rows p // 2 * 128 up to that plus 128 - 1; its column is at most 384. Position 0 has row 0 and column 384; the last position has row 511. `object_field`: each pixel's transmission has magnitude between 0.75 and 1.25.
All inputs are finite; a program needn't handle non-finite values.
Results may differ from the reference program's by a relative error of at most 0.0003.
Values sent between devices are 32-bit elements; how exact they have to be, the bound alone decides.
No kernel may reach another device: no remote copies, remote signals or barrier semaphores. Data moves between devices by JAX's collectives and lax.ppermute only.
A program may use at most 64 MiB of HBM per device.

```python
import math
import jax
import jax.numpy as jnp
from jax import lax

WIN = 128
POS_DEV = 2
STRIP = 128
WIDTH = 512
NSL = 64
ROWS = 512
POSITIONS = 8


def draw_offsets(key, part):
    row_key = jax.random.fold_in(key, 11)
    col_key = jax.random.fold_in(key, 23)
    local_rows = jax.random.randint(row_key, (POSITIONS,), 0, STRIP, dtype=jnp.int32)
    local_rows = local_rows.at[0].set(0).at[POSITIONS - 1].set(STRIP - 1)
    owners = jnp.arange(POSITIONS, dtype=jnp.int32) // POS_DEV
    columns = jax.random.randint(col_key, (POSITIONS,), 0, WIDTH - WIN + 1, dtype=jnp.int32)
    columns = columns.at[0].set(WIDTH - WIN)
    return jnp.stack([owners * STRIP + local_rows, columns], axis=1)


def draw_object_field(key, part):
    amp_key = jax.random.fold_in(key, 31)
    phase_key = jax.random.fold_in(key, 37)
    shape_here = (NSL, ROWS, WIDTH)
    amplitude = jax.random.uniform(amp_key, shape_here, jnp.float32, 0.85, 1.15)
    phase_val = jax.random.uniform(phase_key, shape_here, jnp.float32, -math.pi, math.pi)
    return jnp.stack([amplitude * jnp.cos(phase_val), amplitude * jnp.sin(phase_val)], axis=1)


def block_levels(own_key, shape, pieces, low, high):
    def one(position, parts):
        steps = jax.random.uniform(jax.random.fold_in(jax.random.fold_in(own_key, 6), position), (parts,), jnp.float32, low / len(pieces), high / len(pieces))
        return jnp.repeat(jnp.exp(steps), shape[position] // parts).reshape((-1,) + (1,) * (len(shape) - position - 1))

    loudness = one(*pieces[0])
    for cut in pieces[1:]:
        loudness = loudness * one(*cut)
    return loudness


def scatter_about(stream_key, extent, deviation, reach, held_as=jnp.bfloat16):
    drawn = deviation * jax.random.normal(stream_key, extent, jnp.float32)
    return jnp.clip(drawn, min=-reach, max=reach).astype(held_as)


def setup_inputs(seed: int = 0) -> dict:
    key_of = jax.random.split(jax.random.key(seed), 5)
    return {
        "object_field": draw_object_field(jax.random.fold_in(key_of[4], 71), 0),
        "offsets": draw_offsets(jax.random.fold_in(key_of[4], 71), 0),
        "probe": scatter_about(key_of[2], (2, WIN, WIN), 0.7, 4.2, jnp.float32),
        "intensity": jnp.clip(2.0 * jax.random.uniform(key_of[3], (POSITIONS, WIN, WIN), jnp.float32) ** block_levels(key_of[3], (POSITIONS, WIN, WIN), ((0, 4),), -0.2, 0.2), 0.0, 2.0),
    }


def dft_tables(window, conjugate):
    indices = jnp.arange(window, dtype=jnp.int32)
    product = indices[:, None] * indices[None, :] % window
    angles = product.astype(jnp.float32) * (2.0 * math.pi / window)
    scaling = 1.0 / math.sqrt(window)
    sign_value = 1.0 if conjugate else -1.0
    real_part = jnp.cos(angles) * scaling
    imag_part = sign_value * jnp.sin(angles) * scaling
    right_table = jnp.stack([jnp.stack([real_part, imag_part], 1), jnp.stack([-imag_part, real_part], 1)], 0)
    left_table = jnp.stack([jnp.stack([real_part, -imag_part], 0), jnp.stack([imag_part, real_part], 0)], 0)
    return (right_table, left_table)

def make_tables(window):
    right_fwd, left_fwd = dft_tables(window, False)
    right_inv, left_inv = dft_tables(window, True)
    indices = jnp.arange(window, dtype=jnp.int32)
    centred = (indices + window // 2) % window - window // 2
    squares = centred[:, None] * centred[:, None] + centred[None, :] * centred[None, :]
    phase = squares.astype(jnp.float32) * (math.pi / window)
    return (right_fwd, left_fwd, right_inv, left_inv, jnp.cos(phase), jnp.sin(phase))

def right_product(field, table):
    return jnp.einsum('pcik,ckdj->pdij', field, table, precision=lax.Precision.HIGHEST)

def left_product(table, field):
    return jnp.einsum('dcik,pckj->pdij', table, field, precision=lax.Precision.HIGHEST)

def complex_times(first_re, first_im, second_re, second_im):
    return (first_re * second_re - first_im * second_im, first_re * second_im + first_im * second_re)

def conj_times(first_re, first_im, second_re, second_im):
    return (first_re * second_re + first_im * second_im, first_im * second_re - first_re * second_im)

def as_wave(real_part, imag_part):
    return jnp.stack([real_part, imag_part], 1)

def propagate(field_in, windows, tables):
    right_fwd, left_fwd, right_inv, left_inv, phase_cos, phase_sin = tables
    mixed = as_wave(*complex_times(field_in[:, 0], field_in[:, 1], windows[:, 0], windows[:, 1]))
    across = right_product(mixed, right_fwd)
    spectrum = left_product(left_fwd, across)
    phased = as_wave(*conj_times(spectrum[:, 0], spectrum[:, 1], phase_cos, phase_sin))
    turned = right_product(phased, right_inv)
    return left_product(left_inv, turned)

def adjoint(field_in, windows, grad_out, tables):
    right_fwd, left_fwd, right_inv, left_inv, phase_cos, phase_sin = tables
    grad_last = left_product(left_fwd, grad_out)
    grad_spec = right_product(grad_last, right_fwd)
    grad_phased = as_wave(*complex_times(grad_spec[:, 0], grad_spec[:, 1], phase_cos, phase_sin))
    grad_across = left_product(left_inv, grad_phased)
    grad_mixed = right_product(grad_across, right_inv)
    grad_windows = jnp.stack(conj_times(grad_mixed[:, 0], grad_mixed[:, 1], field_in[:, 0], field_in[:, 1]), 1)
    grad_field = as_wave(*conj_times(grad_mixed[:, 0], grad_mixed[:, 1], windows[:, 0], windows[:, 1]))
    return (grad_field, grad_windows)

def far_field(exit_wave, measured, tables):
    right_fwd, left_fwd, right_inv, left_inv, phase_cos, phase_sin = tables
    across = right_product(exit_wave, right_fwd)
    spectrum = left_product(left_fwd, across)
    power = spectrum[:, 0] * spectrum[:, 0] + spectrum[:, 1] * spectrum[:, 1]
    misfit = power - measured
    weighted = as_wave(misfit * spectrum[:, 0], misfit * spectrum[:, 1])
    grad_across = left_product(left_inv, weighted)
    return right_product(grad_across, right_inv)

def reference(object_field, offsets, probe, intensity):
    tables = make_tables(WIN)
    rows_total = object_field.shape[2]
    window_index = jnp.arange(WIN, dtype=jnp.int32)

    def one_position(grad_total, item):
        offset_pair, measured = item
        row_ids = (offset_pair[0] + window_index) % rows_total
        col_ids = offset_pair[1] + window_index
        patches = object_field[:, :, row_ids[:, None], col_ids[None, :]]

        def forward_step(field_in, windows):
            return (propagate(field_in, windows[None], tables), field_in)
        exit_wave, entries = lax.scan(forward_step, probe[None], patches)
        grad_exit = far_field(exit_wave, measured[None], tables)

        def backward_step(grad_field, pair):
            field_in, windows = pair
            grad_prev, grad_windows = adjoint(field_in, windows[None], grad_field, tables)
            return (grad_prev, grad_windows[0])
        unused, grad_patches = lax.scan(backward_step, grad_exit, (entries, patches), reverse=True)
        grad_total = grad_total.at[:, :, row_ids[:, None], col_ids[None, :]].add(grad_patches)
        return (grad_total, None)
    total, unused = lax.scan(one_position, jnp.zeros(object_field.shape, jnp.float32), (offsets, intensity))
    return total
```

```python
import math

import jax
import jax.numpy as jnp
import ml_dtypes
import numpy as np
from jax import lax
from jax.experimental import pallas as pl
from jax.experimental.pallas import tpu as pltpu
from jax.sharding import PartitionSpec as P

N = 128
CORES = 2
RING = 4
STAGES = 4
PER_DEVICE = 2
PER_CHIP = CORES * PER_DEVICE
PER_STAGE = RING * PER_CHIP
PLANE = (2, N, N)
F32 = jnp.float32
BF16 = jnp.bfloat16
PARAMS = pltpu.CompilerParams(vmem_limit_bytes=40 << 20)


def halves(table):
    high = table.astype(ml_dtypes.bfloat16)
    low = (table - high.astype(np.float64)).astype(ml_dtypes.bfloat16)
    return high, low


def rounded(table):
    scaled = table
    for _ in range(4):
        high, low = halves(scaled)
        total = high.astype(np.float64) + low.astype(np.float64)
        scaled = scaled * (1.0 + np.sum(table * (table - total)) / np.sum(table * table))
    return halves(scaled)


def operator_tables(matrix):
    real, imag = matrix.real, matrix.imag
    right = np.block([[real, imag], [-imag, real]])
    left = np.block([[real, -imag], [imag, real]])
    return rounded(right) + rounded(left)


def make_tables():
    index = np.arange(N)
    product = np.outer(index, index) % N
    dft = np.exp(-2j * np.pi * product / N) / math.sqrt(N)
    centred = (index + N // 2) % N - N // 2
    phase = np.exp(-1j * np.pi * centred * centred / N)
    step = (np.conj(dft) * phase[None, :]) @ dft
    step = (step + step.T) / 2
    return operator_tables(step), operator_tables(dft)


def split(value):
    high = value.astype(BF16)
    return high, (value - high.astype(F32)).astype(BF16)


def product(first, second):
    return jnp.dot(first, second, preferred_element_type=F32)


def two_sided(real, imag, tables):
    right_high, right_low, left_high, left_low = tables
    high, low = split(jnp.concatenate([real, imag], axis=1))
    turned = product(high, right_high[...]) + product(low, right_high[...])
    turned = turned + product(high, right_low[...])
    high, low = split(jnp.concatenate([turned[:, :N], turned[:, N:]], axis=0))
    result = product(left_high[...], high) + product(left_high[...], low)
    result = result + product(left_low[...], high)
    return result[:N], result[N:]


def times(first_re, first_im, second_re, second_im):
    return (
        first_re * second_re - first_im * second_im,
        first_re * second_im + first_im * second_re,
    )


def cut_kernel(where, field, probe, fore_same, fore_other, own_same, own_other, wave):
    lane = lax.broadcasted_iota(jnp.int32, (N, N), 1)

    def cut(target, base):
        tile = pl.multiple_of(where[base + 1] * N, N)
        after = pl.multiple_of(where[base + 2] * N, N)
        wrapped = lane < where[base + 3]
        for layer in range(PER_DEVICE):
            for part in range(2):
                here = field[layer, part, :, pl.ds(tile, N)]
                there = field[layer, part, :, pl.ds(after, N)]
                target[layer, part] = jnp.where(wrapped, there, here)

    cut(own_same, 0)
    cut(own_other, 4)
    cut(fore_same, 8)
    cut(fore_other, 12)
    for part in range(2):
        rolled = pltpu.roll(probe[part], where[0], 0)
        wave[part] = pltpu.roll(rolled, where[3], 1)


def cut_windows(where, field, probe):
    piece = jax.ShapeDtypeStruct((PER_DEVICE,) + PLANE, F32)
    return pl.pallas_call(
        cut_kernel,
        out_shape=(piece,) * 4 + (jax.ShapeDtypeStruct(PLANE, F32),),
        in_specs=[
            pl.BlockSpec(memory_space=pltpu.SMEM),
            pl.BlockSpec(memory_space=pltpu.VMEM),
            pl.BlockSpec(memory_space=pltpu.VMEM),
        ],
        name="cut_windows",
        compiler_params=PARAMS,
    )(where, field, probe)


def paste_kernel(where, own_same, own_other, prev_same, prev_other, out):
    row = lax.broadcasted_iota(jnp.int32, (N, N), 0)
    lane = lax.broadcasted_iota(jnp.int32, (N, N), 1)
    out[...] = jnp.zeros(out.shape, F32)

    def paste(source, base, ahead):
        tile = pl.multiple_of(where[base + 1] * N, N)
        after = pl.multiple_of(where[base + 2] * N, N)
        rows = row < where[base] if ahead else row >= where[base]
        first = rows & (lane >= where[base + 3])
        second = rows & (lane < where[base + 3])
        for layer in range(PER_DEVICE):
            for part in range(2):
                value = source[layer, part]
                out[layer, part, :, pl.ds(tile, N)] += jnp.where(first, value, 0.0)
                out[layer, part, :, pl.ds(after, N)] += jnp.where(second, value, 0.0)

    paste(own_same, 0, False)
    paste(own_other, 4, False)
    paste(prev_same, 8, True)
    paste(prev_other, 12, True)


def paste_windows(where, pieces, shape):
    vmem = pl.BlockSpec(memory_space=pltpu.VMEM)
    return pl.pallas_call(
        paste_kernel,
        out_shape=jax.ShapeDtypeStruct(shape, F32),
        in_specs=[pl.BlockSpec(memory_space=pltpu.SMEM)] + [vmem] * 4,
        name="paste_windows",
        compiler_params=PARAMS,
    )(where, *pieces)


def fetch(place, sources, windows, sems):
    near, up, far_up, far_down, down = sources
    for distance in range(RING):
        chip = (place[1] + distance) % RING
        for slot in range(PER_CHIP):
            if distance == 2:
                source = (far_up if slot < PER_DEVICE else far_down).at[slot % PER_DEVICE]
            else:
                source = (near, up, None, down)[distance].at[slot]
            core = place[2] if slot < PER_DEVICE else 1 - place[2]
            layer = chip * PER_CHIP + core * PER_DEVICE + slot % PER_DEVICE
            pltpu.make_async_copy(source, windows.at[layer], sems.at[layer]).start()


def arrive(source, windows, sems, layer):
    pltpu.make_async_copy(source, windows.at[layer], sems.at[layer]).wait()


def forward_steps(count, real, imag, windows, history, sems, source, tables):
    def one(layer, state):
        real, imag = state
        arrive(source, windows, sems, layer)
        history[layer, 0] = real
        history[layer, 1] = imag
        mixed = times(real, imag, windows[layer, 0], windows[layer, 1])
        return two_sided(*mixed, tables)

    return lax.fori_loop(0, count, one, (real, imag), unroll=count // 5 if count % 5 == 0 else 4)


def forward_kernel(place, near, up, far_up, far_down, down, wave, *rest):
    tables, (leaving, saved, windows, history, sems, out_sem) = rest[:4], rest[4:]

    @pl.when(place[0] == 1)
    def _():
        fetch(place, (near, up, far_up, far_down, down), windows, sems)
        real, imag = forward_steps(
            PER_STAGE, wave[0], wave[1], windows, history, sems, near.at[0], tables
        )
        leaving[0] = real
        leaving[1] = imag
        kept = history.at[pl.ds(place[1] * PER_CHIP, PER_CHIP)]
        copy = pltpu.make_async_copy(kept, saved, out_sem)
        copy.start()
        copy.wait()


def gradients(place, trail, psi_of, piece, same, other, sems):
    for slot in range(PER_CHIP):
        core = place[2] if slot < PER_DEVICE else 1 - place[2]
        local = core * PER_DEVICE + slot % PER_DEVICE
        layer = place[1] * PER_CHIP + local
        psi_re, psi_im = psi_of(layer, local)
        real, imag = times(trail[layer, 0], trail[layer, 1], psi_re, psi_im)
        piece[slot, 0] = real
        piece[slot, 1] = -imag
    copies = (
        pltpu.make_async_copy(piece.at[pl.ds(0, PER_DEVICE)], same, sems.at[0]),
        pltpu.make_async_copy(piece.at[pl.ds(PER_DEVICE, PER_DEVICE)], other, sems.at[1]),
    )
    for copy in copies:
        copy.start()
    for copy in copies:
        copy.wait()


def backward_kernel(place, near, up, far_up, far_down, down, wave, saved, *rest):
    tables, rest = rest[:4], rest[4:]
    unused_same, unused_other, leaving, same, other, windows, trail, psi, piece, sems, more = rest

    @pl.when(place[0] == 1)
    def _():
        fetch(place, (near, up, far_up, far_down, down), windows, sems)
        load = pltpu.make_async_copy(saved, psi, more.at[2])
        load.start()

        def one(step, state):
            layer = PER_STAGE - 1 - step
            real, imag = state
            arrive(near.at[0], windows, sems, layer)
            trail[layer, 0] = real
            trail[layer, 1] = imag
            mixed = times(real, imag, windows[layer, 0], windows[layer, 1])
            return two_sided(*mixed, tables)

        real, imag = lax.fori_loop(0, PER_STAGE, one, (wave[0], wave[1]), unroll=4)
        leaving[0] = real
        leaving[1] = imag
        load.wait()
        gradients(
            place,
            trail,
            lambda layer, local: (psi[local, 0], psi[local, 1]),
            piece,
            same,
            other,
            more,
        )


def turn_kernel(place, near, up, far_up, far_down, down, wave, measured, *rest):
    tables, far_tables, rest = rest[:4], rest[4:8], rest[8:]
    leaving, same, other, windows, history, trail, piece, sems, more = rest

    @pl.when(place[0] == 1)
    def _():
        fetch(place, (near, up, far_up, far_down, down), windows, sems)
        last = PER_STAGE - 1
        real, imag = forward_steps(
            last, wave[0], wave[1], windows, history, sems, near.at[0], tables
        )
        arrive(near.at[0], windows, sems, last)
        history[last, 0] = real
        history[last, 1] = imag
        mixed = times(real, imag, windows[last, 0], windows[last, 1])
        real, imag = two_sided(*mixed, far_tables)
        misfit = real * real + imag * imag - measured[...]
        real, imag = two_sided(misfit * real, -(misfit * imag), far_tables)

        def one(step, state):
            layer = last - step
            real, imag = state
            trail[layer, 0] = real
            trail[layer, 1] = imag
            mixed = times(real, imag, windows[layer, 0], windows[layer, 1])
            return two_sided(*mixed, tables)

        real, imag = lax.fori_loop(0, PER_STAGE, one, (real, imag), unroll=4)
        leaving[0] = real
        leaving[1] = imag
        gradients(
            place,
            trail,
            lambda layer, local: (history[layer, 0], history[layer, 1]),
            piece,
            same,
            other,
            more,
        )


STACK = pltpu.VMEM((PER_STAGE,) + PLANE, F32)
CHIP_STACK = pltpu.VMEM((PER_CHIP,) + PLANE, F32)
WAVE = jax.ShapeDtypeStruct(PLANE, F32)
PIECE = jax.ShapeDtypeStruct((PER_DEVICE,) + PLANE, F32)
SAVED = jax.ShapeDtypeStruct((PER_CHIP,) + PLANE, F32)
SMEM_SPEC = pl.BlockSpec(memory_space=pltpu.SMEM)
VMEM_SPEC = pl.BlockSpec(memory_space=pltpu.VMEM)
ANY_SPEC = pl.BlockSpec(memory_space=pl.ANY)


def forward_stage(place, sources, wave, tables):
    return pl.pallas_call(
        forward_kernel,
        out_shape=(WAVE, SAVED),
        in_specs=[SMEM_SPEC] + [ANY_SPEC] * 5 + [VMEM_SPEC] * 5,
        out_specs=(VMEM_SPEC, ANY_SPEC),
        scratch_shapes=[
            STACK,
            STACK,
            pltpu.SemaphoreType.DMA((PER_STAGE,)),
            pltpu.SemaphoreType.DMA(()),
        ],
        name="forward_stage",
        compiler_params=PARAMS,
    )(place, *sources, wave, *tables)


def backward_stage(place, sources, wave, saved, tables, same, other):
    return pl.pallas_call(
        backward_kernel,
        out_shape=(WAVE, PIECE, PIECE),
        in_specs=[SMEM_SPEC] + [ANY_SPEC] * 5 + [VMEM_SPEC, ANY_SPEC] + [VMEM_SPEC] * 4
        + [ANY_SPEC] * 2,
        out_specs=(VMEM_SPEC, ANY_SPEC, ANY_SPEC),
        scratch_shapes=[
            STACK,
            STACK,
            CHIP_STACK,
            CHIP_STACK,
            pltpu.SemaphoreType.DMA((PER_STAGE,)),
            pltpu.SemaphoreType.DMA((3,)),
        ],
        input_output_aliases={12: 1, 13: 2},
        name="backward_stage",
        compiler_params=PARAMS,
    )(place, *sources, wave, saved, *tables, same, other)


def turn_stage(place, sources, wave, measured, tables, far_tables):
    return pl.pallas_call(
        turn_kernel,
        out_shape=(WAVE, PIECE, PIECE),
        in_specs=[SMEM_SPEC] + [ANY_SPEC] * 5 + [VMEM_SPEC] * 10,
        out_specs=(VMEM_SPEC, ANY_SPEC, ANY_SPEC),
        scratch_shapes=[
            STACK,
            STACK,
            STACK,
            CHIP_STACK,
            pltpu.SemaphoreType.DMA((PER_STAGE,)),
            pltpu.SemaphoreType.DMA((2,)),
        ],
        name="turn_stage",
        compiler_params=PARAMS,
    )(place, *sources, wave, measured, *tables, *far_tables)


def along_ring(value, steps):
    def target(device):
        stage, rest = divmod(device, RING * CORES)
        chip, core = divmod(rest, CORES)
        return (stage * RING + (chip + steps) % RING) * CORES + core

    pairs = [(device, target(device)) for device in range(STAGES * RING * CORES)]
    return lax.ppermute(value, "depth", pairs)


def along_stages(value, steps):
    count = STAGES * RING * CORES
    pairs = [(device, (device + steps * RING * CORES) % count) for device in range(count)]
    return lax.ppermute(value, "depth", pairs)


def across(value, strips, swap):
    rows, depth = lax.axis_size("pos"), lax.axis_size("depth")
    pairs = []
    for strip in range(rows):
        for device in range(depth):
            other = device ^ 1 if swap else device
            pairs.append((strip * depth + device, (strip + strips) % rows * depth + other))
    return lax.ppermute(value, ("pos", "depth"), pairs)


def corner(offsets, strip_rows):
    tile = offsets[:, 1] // N
    after = jnp.minimum(tile + 1, 3)
    return jnp.stack([offsets[:, 0] % strip_rows, tile, after, offsets[:, 1] % N], axis=1)


def body(object_field, offsets, probe, intensity, tables, far_tables):
    strip_rows = object_field.shape[2]
    depth_here = lax.axis_index("depth")
    core = depth_here % CORES
    chip = depth_here // CORES % RING
    stage = depth_here // (CORES * RING)

    rows, depth = lax.axis_size("pos"), lax.axis_size("depth")
    before = lax.ppermute(offsets, "pos", [(i, (i + 1) % rows) for i in range(rows)])
    own = corner(offsets, strip_rows)
    prev = corner(before, strip_rows)
    flip = core == 1
    own = jnp.where(flip, own[::-1], own)
    prev = jnp.where(flip, prev[::-1], prev)
    where = jnp.concatenate([own.reshape(-1), prev.reshape(-1)])

    fore_same, fore_other, own_same, own_other, wave = cut_windows(where, object_field, probe)
    fore_same = across(fore_same, -1, False)
    fore_other = across(fore_other, -1, True)
    own_other = across(own_other, 0, True)
    below = jnp.arange(strip_rows, dtype=jnp.int32)[:, None] >= where[0]
    near = jnp.concatenate(
        [jnp.where(below, own_same, fore_same), jnp.where(below, own_other, fore_other)], axis=0
    )
    up = along_ring(near, -1)
    down = along_ring(near, 1)
    far_up = along_ring(up[:PER_DEVICE], -1)
    far_down = along_ring(down[PER_DEVICE:], 1)
    sources = (near, up, far_up, far_down, down)

    def place(section):
        return jnp.stack([(stage == section).astype(jnp.int32), chip, core])

    kept = []
    for section in range(STAGES - 1):
        wave, saved = forward_stage(place(section), sources, wave, tables)
        kept.append(saved)
        wave = along_stages(wave, 1)
    measured = lax.dynamic_index_in_dim(intensity, core, 0, keepdims=False)
    wave, same, other = turn_stage(
        place(STAGES - 1), sources, wave, measured, tables, far_tables
    )
    for section in reversed(range(STAGES - 1)):
        wave = along_stages(wave, -1)
        wave, same, other = backward_stage(
            place(section), sources, wave, kept[section], tables, same, other
        )
    prev_same = across(same, 1, False)
    prev_other = across(other, 1, True)
    own_other = across(other, 0, True)
    return paste_windows(where, (same, own_other, prev_same, prev_other), object_field.shape)


def solution(mesh):
    step, far = make_tables()
    mapped = jax.shard_map(
        body,
        mesh=mesh,
        in_specs=(
            P("depth", None, "pos", None),
            P("pos", None),
            P(),
            P("pos", None, None),
            P(),
            P(),
        ),
        out_specs=P("depth", None, "pos", None),
        check_vma=False,
    )

    def run(object_field, offsets, probe, intensity):
        return mapped(
            object_field,
            offsets,
            probe,
            intensity,
            tuple(jnp.asarray(table) for table in step),
            tuple(jnp.asarray(table) for table in far),
        )

    return run
```

```python
import functools
import math

import jax
import jax.numpy as jnp
import numpy as np
from jax import lax
from jax.experimental import pallas as pl
from jax.experimental.pallas import tpu as pltpu
from jax.sharding import PartitionSpec as P

N = 128
CORES = 2
RING = 4
STAGES = 4
PER_DEVICE = 2
PER_CHIP = CORES * PER_DEVICE
PER_STAGE = RING * PER_CHIP
PLANE = (2, N, N)
F32 = jnp.float32
PARAMS = pltpu.CompilerParams(vmem_limit_bytes=40 << 20)
GROUP = 8
STACK = pltpu.VMEM((PER_STAGE,) + PLANE, F32)
CHIP_STACK = pltpu.VMEM((PER_CHIP,) + PLANE, F32)
ROW_STAGES = pltpu.VMEM((2,) + PLANE, F32)
WAVE = jax.ShapeDtypeStruct(PLANE, F32)
PIECE = jax.ShapeDtypeStruct((PER_DEVICE,) + PLANE, F32)
SAVED = jax.ShapeDtypeStruct((PER_CHIP,) + PLANE, F32)
SMEM_SPEC = pl.BlockSpec(memory_space=pltpu.SMEM)
VMEM_SPEC = pl.BlockSpec(memory_space=pltpu.VMEM)
ANY_SPEC = pl.BlockSpec(memory_space=pl.ANY)


def make_tables():
    index = np.arange(N)
    turn = np.exp(1j * np.pi * (index * index % (2 * N)) / N)
    chirp = np.outer(turn, turn)
    first, second = np.divmod(index, GROUP)
    twiddle = np.exp(-2j * np.pi * first * second / N)[:, None] * np.ones((1, N))
    tables = (
        twiddle,
        -1j * chirp * chirp / N,
        1j * np.conj(chirp),
        np.conj(chirp),
        1j * np.conj(chirp) / N,
        -chirp * chirp,
    )
    return tuple(np.stack([t.real, t.imag]).astype(np.float32) for t in tables)


def times(first_re, first_im, second_re, second_im):
    return (
        first_re * second_re - first_im * second_im,
        first_re * second_im + first_im * second_re,
    )


def rotate(value, numerator, count):
    real, imag = value
    if numerator == 0:
        return value
    if numerator * 4 == count:
        return imag, -real
    half = math.sqrt(0.5)
    if numerator * 8 == count:
        return (real + imag) * half, (imag - real) * half
    if numerator * 8 == 3 * count:
        return (imag - real) * half, -(real + imag) * half
    cosine = math.cos(2.0 * math.pi * numerator / count)
    sine = -math.sin(2.0 * math.pi * numerator / count)
    return real * cosine - imag * sine, real * sine + imag * cosine


def transform(values):
    count = len(values)
    if count == 1:
        return values
    even, odd = transform(values[0::2]), transform(values[1::2])
    result = [None] * count
    for k in range(count // 2):
        moved = rotate(odd[k], k, count)
        result[k] = (even[k][0] + moved[0], even[k][1] + moved[1])
        result[k + count // 2] = (even[k][0] - moved[0], even[k][1] - moved[1])
    return result


def transform_rows(real, imag, twiddle, stage):
    groups = [
        (real[GROUP * k : GROUP * (k + 1)], imag[GROUP * k : GROUP * (k + 1)])
        for k in range(N // GROUP)
    ]
    for k, value in enumerate(transform(groups)):
        rows = pl.ds(GROUP * k, GROUP)
        if k:
            value = times(*value, twiddle[0, rows], twiddle[1, rows])
        stage[0, rows], stage[1, rows] = value
    result = [None] * (N // GROUP)
    for part in range(2):
        picked = [pl.ds(GROUP * GROUP * part + k, GROUP, stride=GROUP) for k in range(GROUP)]
        done = transform([(stage[0, rows], stage[1, rows]) for rows in picked])
        for k in range(GROUP):
            result[2 * k + part] = done[k]
    return (
        jnp.concatenate([value[0] for value in result], axis=0),
        jnp.concatenate([value[1] for value in result], axis=0),
    )


def two_sided(real, imag, twiddle, stages):
    real, imag = transform_rows(real, imag, twiddle, stages.at[0])
    return transform_rows(real.T, imag.T, twiddle, stages.at[1])


def cut(where, base, field, factor, target):
    lane = lax.broadcasted_iota(jnp.int32, (N, N), 1)
    tile = pl.multiple_of(where[base + 1] * N, N)
    after = pl.multiple_of(where[base + 2] * N, N)
    wrapped = lane < where[base + 3]
    for layer in range(PER_DEVICE):
        value = [
            jnp.where(
                wrapped,
                field[layer, part, :, pl.ds(after, N)],
                field[layer, part, :, pl.ds(tile, N)],
            )
            for part in range(2)
        ]
        value = times(*value, factor[0], factor[1])
        for part in range(2):
            target[layer, part] = value[part].T if layer % 2 else value[part]


def cut_fore_kernel(where, field, factor, same, other):
    cut(where, 8, field, factor, same)
    cut(where, 12, field, factor, other)


def cut_own_kernel(where, field, factor, probe, start, same, other, wave):
    cut(where, 0, field, factor, same)
    cut(where, 4, field, factor, other)
    rolled = [pltpu.roll(pltpu.roll(probe[k], where[0], 0), where[3], 1) for k in range(2)]
    wave[0], wave[1] = times(*rolled, start[0], start[1])


def cut_fore(where, field, factor):
    return pl.pallas_call(
        cut_fore_kernel,
        out_shape=(PIECE, PIECE),
        in_specs=[SMEM_SPEC] + [VMEM_SPEC] * 2,
        name="cut_fore",
        compiler_params=PARAMS,
    )(where, field, factor)


def cut_own(where, field, factor, probe, start):
    return pl.pallas_call(
        cut_own_kernel,
        out_shape=(PIECE, PIECE, WAVE),
        in_specs=[SMEM_SPEC] + [VMEM_SPEC] * 4,
        name="cut_own",
        compiler_params=PARAMS,
    )(where, field, factor, probe, start)


def paste_kernel(where, own_same, own_other, prev_same, prev_other, out):
    row = lax.broadcasted_iota(jnp.int32, (N, N), 0)
    lane = lax.broadcasted_iota(jnp.int32, (N, N), 1)
    out[...] = jnp.zeros(out.shape, F32)

    def paste(source, base, ahead):
        tile = pl.multiple_of(where[base + 1] * N, N)
        after = pl.multiple_of(where[base + 2] * N, N)
        rows = row < where[base] if ahead else row >= where[base]
        first = rows & (lane >= where[base + 3])
        second = rows & (lane < where[base + 3])
        for layer in range(PER_DEVICE):
            for part in range(2):
                value = source[layer, part]
                out[layer, part, :, pl.ds(tile, N)] += jnp.where(first, value, 0.0)
                out[layer, part, :, pl.ds(after, N)] += jnp.where(second, value, 0.0)

    paste(own_same, 0, False)
    paste(own_other, 4, False)
    paste(prev_same, 8, True)
    paste(prev_other, 12, True)


def paste_windows(where, pieces, shape):
    return pl.pallas_call(
        paste_kernel,
        out_shape=jax.ShapeDtypeStruct(shape, F32),
        in_specs=[SMEM_SPEC] + [VMEM_SPEC] * 4,
        name="paste_windows",
        compiler_params=PARAMS,
    )(where, *pieces)


def fetch(place, sources, windows, sems):
    near, up, far_up, far_down, down = sources
    for distance in range(RING):
        chip = (place[1] + distance) % RING
        for slot in range(PER_CHIP):
            if distance == 2:
                source = (far_up if slot < PER_DEVICE else far_down).at[slot % PER_DEVICE]
            else:
                source = (near, up, None, down)[distance].at[slot]
            core = place[2] if slot < PER_DEVICE else 1 - place[2]
            layer = chip * PER_CHIP + core * PER_DEVICE + slot % PER_DEVICE
            pltpu.make_async_copy(source, windows.at[layer], sems.at[layer]).start()


def arrive(source, windows, sems, layer):
    pltpu.make_async_copy(source, windows.at[layer], sems.at[layer]).wait()


def steps(first, count, change, state, windows, trail, sems, source, twiddle, stages):
    def one(step, state):
        layer = first + change * step
        real, imag = state
        if sems is not None:
            arrive(source, windows, sems, layer)
        trail[layer, 0] = real
        trail[layer, 1] = imag
        mixed = times(real, imag, windows[layer, 0], windows[layer, 1])
        return two_sided(*mixed, twiddle, stages)

    return lax.fori_loop(0, count, one, state)


def forward_kernel(section, place, near, up, far_up, far_down, down, wave, twiddle, *rest):
    leaving, saved, windows, trail, stages, sems, out_sem = rest

    @pl.when(place[0] == section)
    def _():
        fetch(place, (near, up, far_up, far_down, down), windows, sems)
        leaving[0], leaving[1] = steps(
            0, PER_STAGE, 1, (wave[0], wave[1]), windows, trail, sems, near.at[0], twiddle, stages
        )
        kept = trail.at[pl.ds(place[1] * PER_CHIP, PER_CHIP)]
        copy = pltpu.make_async_copy(kept, saved, out_sem)
        copy.start()
        copy.wait()


def gradients(place, trail, psi_of, factor, piece, same, other, sems):
    for slot in range(PER_CHIP):
        core = place[2] if slot < PER_DEVICE else 1 - place[2]
        local = core * PER_DEVICE + slot % PER_DEVICE
        layer = place[1] * PER_CHIP + local
        psi_re, psi_im = psi_of(layer, local)
        value = times(trail[layer, 0], trail[layer, 1], psi_re, psi_im)
        real, imag = times(*value, factor[0], factor[1])
        piece[slot, 0] = real.T if slot % 2 else real
        piece[slot, 1] = (-imag).T if slot % 2 else -imag
    copies = (
        pltpu.make_async_copy(piece.at[pl.ds(0, PER_DEVICE)], same, sems.at[0]),
        pltpu.make_async_copy(piece.at[pl.ds(PER_DEVICE, PER_DEVICE)], other, sems.at[1]),
    )
    for copy in copies:
        copy.start()
    for copy in copies:
        copy.wait()


def backward_kernel(section, place, near, up, far_up, far_down, down, wave, saved, *rest):
    twiddle, factor, unused_same, unused_other, leaving, same, other = rest[:7]
    windows, trail, psi, piece, stages, sems, more = rest[7:]

    @pl.when(place[0] == section)
    def _():
        fetch(place, (near, up, far_up, far_down, down), windows, sems)
        load = pltpu.make_async_copy(saved, psi, more.at[2])
        load.start()
        state = (wave[0], wave[1])
        last = PER_STAGE - 1
        leaving[0], leaving[1] = steps(
            last, PER_STAGE, -1, state, windows, trail, sems, near.at[0], twiddle, stages
        )
        load.wait()
        gradients(
            place,
            trail,
            lambda layer, local: (psi[local, 0], psi[local, 1]),
            factor,
            piece,
            same,
            other,
            more,
        )


def turn_kernel(section, place, near, up, far_up, far_down, down, wave, measured, *rest):
    twiddle, factor, into, back, leaving, same, other = rest[:7]
    windows, history, trail, piece, stages, sems, more = rest[7:]

    @pl.when(place[0] == section)
    def _():
        fetch(place, (near, up, far_up, far_down, down), windows, sems)
        last = PER_STAGE - 1
        source = near.at[0]
        state = (wave[0], wave[1])
        state = steps(0, last, 1, state, windows, history, sems, source, twiddle, stages)
        arrive(source, windows, sems, last)
        history[last, 0], history[last, 1] = state
        mixed = times(*state, windows[last, 0], windows[last, 1])
        real, imag = two_sided(*times(*mixed, into[0], into[1]), twiddle, stages)
        misfit = real * real + imag * imag - measured[...]
        state = two_sided(misfit * real, -(misfit * imag), twiddle, stages)
        state = times(*state, back[0], back[1])
        leaving[0], leaving[1] = steps(
            last, PER_STAGE, -1, state, windows, trail, None, source, twiddle, stages
        )
        gradients(
            place,
            trail,
            lambda layer, local: (history[layer, 0], history[layer, 1]),
            factor,
            piece,
            same,
            other,
            more,
        )


def forward_stage(section, place, sources, wave, twiddle):
    return pl.pallas_call(
        functools.partial(forward_kernel, section),
        out_shape=(WAVE, SAVED),
        in_specs=[SMEM_SPEC] + [ANY_SPEC] * 5 + [VMEM_SPEC] * 2,
        out_specs=(VMEM_SPEC, ANY_SPEC),
        scratch_shapes=[
            STACK,
            STACK,
            ROW_STAGES,
            pltpu.SemaphoreType.DMA((PER_STAGE,)),
            pltpu.SemaphoreType.DMA(()),
        ],
        name="forward_stage",
        compiler_params=PARAMS,
    )(place, *sources, wave, twiddle)


def backward_stage(section, place, sources, wave, saved, twiddle, factor, same, other):
    return pl.pallas_call(
        functools.partial(backward_kernel, section),
        out_shape=(WAVE, PIECE, PIECE),
        in_specs=[SMEM_SPEC] + [ANY_SPEC] * 5 + [VMEM_SPEC, ANY_SPEC] + [VMEM_SPEC] * 2
        + [ANY_SPEC] * 2,
        out_specs=(VMEM_SPEC, ANY_SPEC, ANY_SPEC),
        scratch_shapes=[
            STACK,
            STACK,
            CHIP_STACK,
            CHIP_STACK,
            ROW_STAGES,
            pltpu.SemaphoreType.DMA((PER_STAGE,)),
            pltpu.SemaphoreType.DMA((3,)),
        ],
        input_output_aliases={10: 1, 11: 2},
        name="backward_stage",
        compiler_params=PARAMS,
    )(place, *sources, wave, saved, twiddle, factor, same, other)


def turn_stage(section, place, sources, wave, measured, twiddle, factor, into, back):
    return pl.pallas_call(
        functools.partial(turn_kernel, section),
        out_shape=(WAVE, PIECE, PIECE),
        in_specs=[SMEM_SPEC] + [ANY_SPEC] * 5 + [VMEM_SPEC] * 6,
        out_specs=(VMEM_SPEC, ANY_SPEC, ANY_SPEC),
        scratch_shapes=[
            STACK,
            STACK,
            STACK,
            CHIP_STACK,
            ROW_STAGES,
            pltpu.SemaphoreType.DMA((PER_STAGE,)),
            pltpu.SemaphoreType.DMA((2,)),
        ],
        name="turn_stage",
        compiler_params=PARAMS,
    )(place, *sources, wave, measured, twiddle, factor, into, back)


def along_ring(value, steps):
    def target(device):
        stage, rest = divmod(device, RING * CORES)
        chip, core = divmod(rest, CORES)
        return (stage * RING + (chip + steps) % RING) * CORES + core

    pairs = [(device, target(device)) for device in range(STAGES * RING * CORES)]
    return lax.ppermute(value, "depth", pairs)


def along_stages(value, steps):
    count = STAGES * RING * CORES
    pairs = [(device, (device + steps * RING * CORES) % count) for device in range(count)]
    return lax.ppermute(value, "depth", pairs)


def across(value, strips, swap):
    rows, depth = lax.axis_size("pos"), lax.axis_size("depth")
    pairs = []
    for strip in range(rows):
        for device in range(depth):
            other = device ^ 1 if swap else device
            pairs.append((strip * depth + device, (strip + strips) % rows * depth + other))
    return lax.ppermute(value, ("pos", "depth"), pairs)


def corner(offsets, strip_rows):
    tile = offsets[:, 1] // N
    after = jnp.minimum(tile + 1, 3)
    return jnp.stack([offsets[:, 0] % strip_rows, tile, after, offsets[:, 1] % N], axis=1)


def body(object_field, offsets, probe, intensity, tables):
    twiddle, factor, start, into, back, last_factor = tables
    strip_rows = object_field.shape[2]
    depth_here = lax.axis_index("depth")
    core = depth_here % CORES
    chip = depth_here // CORES % RING
    stage = depth_here // (CORES * RING)
    place = jnp.stack([stage, chip, core])

    rows = lax.axis_size("pos")
    before = lax.ppermute(offsets, "pos", [(i, (i + 1) % rows) for i in range(rows)])
    own = corner(offsets, strip_rows)
    prev = corner(before, strip_rows)
    flip = core == 1
    own = jnp.where(flip, own[::-1], own)
    prev = jnp.where(flip, prev[::-1], prev)
    where = jnp.concatenate([own.reshape(-1), prev.reshape(-1)])

    fore_same, fore_other = cut_fore(where, object_field, factor)
    fore_same = across(fore_same, -1, False)
    fore_other = across(fore_other, -1, True)
    own_same, own_other, wave = cut_own(where, object_field, factor, probe, start)
    own_other = across(own_other, 0, True)
    index = jnp.arange(N, dtype=jnp.int32)
    upright = jnp.broadcast_to(index[:, None] >= where[0], (N, N))
    below = jnp.stack([upright, upright.T])[:, None]
    near = jnp.concatenate(
        [jnp.where(below, own_same, fore_same), jnp.where(below, own_other, fore_other)], axis=0
    )
    up = along_ring(near, -1)
    down = along_ring(near, 1)
    far_up = along_ring(up[:PER_DEVICE], -1)
    far_down = along_ring(down[PER_DEVICE:], 1)
    sources = (near, up, far_up, far_down, down)

    kept = []
    for section in range(STAGES - 1):
        wave, saved = forward_stage(section, place, sources, wave, twiddle)
        kept.append(saved)
        wave = along_stages(wave, 1)
    measured = lax.dynamic_index_in_dim(intensity, core, 0, keepdims=False)
    wave, same, other = turn_stage(
        STAGES - 1, place, sources, wave, measured, twiddle, last_factor, into, back
    )
    for section in reversed(range(STAGES - 1)):
        wave = along_stages(wave, -1)
        wave, same, other = backward_stage(
            section, place, sources, wave, kept[section], twiddle, last_factor, same, other
        )
    prev_same = across(same, 1, False)
    prev_other = across(other, 1, True)
    own_other = across(other, 0, True)
    return paste_windows(where, (same, own_other, prev_same, prev_other), object_field.shape)


def solution(mesh):
    mapped = jax.shard_map(
        body,
        mesh=mesh,
        in_specs=(
            P("depth", None, "pos", None),
            P("pos", None),
            P(),
            P("pos", None, None),
            P(),
        ),
        out_specs=P("depth", None, "pos", None),
        check_vma=False,
    )
    tables = make_tables()

    def run(object_field, offsets, probe, intensity):
        constants = tuple(jnp.asarray(table) for table in tables)
        return mapped(object_field, offsets, probe, intensity, constants)

    return run
```

```python
import functools
import math

import jax
import jax.numpy as jnp
import numpy as np
from jax import lax
from jax.experimental import pallas as pl
from jax.experimental.pallas import tpu as pltpu
from jax.sharding import PartitionSpec as P

N = 128
CORES = 2
RING = 4
STAGES = 4
PER_DEVICE = 2
PER_CHIP = CORES * PER_DEVICE
PER_STAGE = RING * PER_CHIP
PLANE = (2, N, N)
F32 = jnp.float32
PARAMS = pltpu.CompilerParams(vmem_limit_bytes=20 << 20)
GROUP = 8
PAD_ROWS = 128
PITCH = GROUP + 1
TRAIL = pltpu.VMEM((PER_STAGE + 1,) + PLANE, F32)
ROW_STAGES = pltpu.VMEM((2, 2, 160, N), F32)
WAVE = jax.ShapeDtypeStruct(PLANE, F32)
PIECE = jax.ShapeDtypeStruct((PER_DEVICE,) + PLANE, F32)
SAVED = jax.ShapeDtypeStruct((PER_CHIP,) + PLANE, F32)
STACK = jax.ShapeDtypeStruct((PER_STAGE,) + PLANE, F32)
SMEM_SPEC = pl.BlockSpec(memory_space=pltpu.SMEM)
VMEM_SPEC = pl.BlockSpec(memory_space=pltpu.VMEM)
ANY_SPEC = pl.BlockSpec(memory_space=pl.ANY)


def make_tables():
    index = np.arange(N)
    turn = np.exp(1j * np.pi * (index * index % (2 * N)) / N)
    chirp = np.outer(turn, turn)
    first, second = np.divmod(index, GROUP)
    twiddle = np.exp(-2j * np.pi * first * second / N)[:, None] * np.ones((1, N))
    tables = (twiddle, np.conj(chirp))
    return tuple(np.stack([t.real, t.imag]).astype(np.float32) for t in tables)


def times(first_re, first_im, second_re, second_im):
    return (
        first_re * second_re - first_im * second_im,
        first_re * second_im + first_im * second_re,
    )


def rotate(value, numerator, count):
    real, imag = value
    if numerator == 0:
        return value
    if numerator * 4 == count:
        return imag, -real
    half = math.sqrt(0.5)
    if numerator * 8 == count:
        return (real + imag) * half, (imag - real) * half
    if numerator * 8 == 3 * count:
        return (imag - real) * half, -(real + imag) * half
    cosine = math.cos(2.0 * math.pi * numerator / count)
    sine = -math.sin(2.0 * math.pi * numerator / count)
    return real * cosine - imag * sine, real * sine + imag * cosine


def transform(values):
    count = len(values)
    if count == 1:
        return values
    even, odd = transform(values[0::2]), transform(values[1::2])
    result = [None] * count
    for k in range(count // 2):
        moved = rotate(odd[k], k, count)
        result[k] = (even[k][0] + moved[0], even[k][1] + moved[1])
        result[k + count // 2] = (even[k][0] - moved[0], even[k][1] - moved[1])
    return result


def transform_rows(real, imag, twiddle, stage, put):
    groups = [
        (real[GROUP * k : GROUP * (k + 1)], imag[GROUP * k : GROUP * (k + 1)])
        for k in range(N // GROUP)
    ]
    for k, value in enumerate(transform(groups)):
        rows = pl.ds(GROUP * k, GROUP)
        if k:
            value = times(*value, twiddle[0, rows], twiddle[1, rows])
        rows = pl.ds(PITCH * k, GROUP)
        stage[0, rows], stage[1, rows] = value
    for part in range(2):
        picked = [pl.ds(PITCH * GROUP * part + k, GROUP, stride=PITCH) for k in range(GROUP)]
        done = transform([(stage[0, rows], stage[1, rows]) for rows in picked])
        for k in range(GROUP):
            put(2 * k + part, done[k])


def advance(real, imag, target, twiddle, stages):
    rows = [None] * (N // GROUP)
    transform_rows(real, imag, twiddle, stages.at[0], rows.__setitem__)
    real, imag = (jnp.concatenate([row[k] for row in rows], axis=0).T for k in range(2))

    def put(k, value):
        place = pl.ds(GROUP * k, GROUP)
        target[0, place], target[1, place] = value

    transform_rows(real, imag, twiddle, stages.at[1], put)


def corner(offsets, position):
    row = offsets[position, 0]
    column = offsets[position, 1]
    tile = column // N
    after = pl.multiple_of(jnp.minimum(tile + 1, 3) * N, N)
    return row % N, pl.multiple_of(tile * N, N), after, column % N


def squared(chirp):
    real, imag = chirp[0], chirp[1]
    return real * real - imag * imag, -2.0 * real * imag


def cut(offsets, position, field, chirp, targets):
    lane = lax.broadcasted_iota(jnp.int32, (N, N), 1)
    unused, tile, after, shift = corner(offsets, position)
    wrapped = lane < shift
    real, imag = squared(chirp)
    factor = (imag * (1.0 / N), real * (-1.0 / N))
    for layer in range(PER_DEVICE):
        value = [
            jnp.where(
                wrapped,
                field[layer, part, :, pl.ds(after, N)],
                field[layer, part, :, pl.ds(tile, N)],
            )
            for part in range(2)
        ]
        value = times(*value, *factor)
        for part in range(2):
            targets[layer][part] = value[part].T if layer % 2 else value[part]


def here():
    device = lax.axis_index("depth")
    return device // (CORES * RING), device // CORES % RING, device % CORES


def cut_own_kernel(offsets, field, chirp, probe, same0, same1, other, wave, *copies):
    core = here()[2]
    cut(offsets, core, field, chirp, (same0, same1))
    cut(offsets, 1 - core, field, chirp, [other.at[k] for k in range(PER_DEVICE)])
    row, unused, unused, shift = corner(offsets, core)
    rolled = [pltpu.roll(pltpu.roll(probe[k], row, 0), shift, 1) for k in range(2)]
    real, imag = times(*rolled, chirp[0], chirp[1])
    wave[0] = -imag
    wave[1] = real
    copies[0][...] = field[...]
    copies[1][...] = chirp[...]


def cut_fore_kernel(before, field, chirp, *targets):
    core = here()[2]
    cut(before, core, field, chirp, targets[:2])
    cut(before, 1 - core, field, chirp, targets[2:])


def cut_own(offsets, field, chirp, probe):
    return pl.pallas_call(
        cut_own_kernel,
        out_shape=(WAVE, WAVE, PIECE, WAVE, jax.ShapeDtypeStruct(field.shape, F32), WAVE),
        in_specs=[SMEM_SPEC] + [VMEM_SPEC] * 3,
        name="cut_own",
        compiler_params=PARAMS,
    )(offsets, field, chirp, probe)


def cut_fore(before, field, chirp):
    return pl.pallas_call(
        cut_fore_kernel,
        out_shape=(WAVE,) * 4,
        in_specs=[SMEM_SPEC] + [VMEM_SPEC] * 2,
        name="cut_fore",
        compiler_params=PARAMS,
    )(before, field, chirp)


def paste(offsets, position, value, target, ahead):
    row = lax.broadcasted_iota(jnp.int32, (N, N), 0)
    lane = lax.broadcasted_iota(jnp.int32, (N, N), 1)
    top, tile, after, shift = corner(offsets, position)
    rows = row < top if ahead else row >= top
    target[:, pl.ds(tile, N)] += jnp.where(rows & (lane >= shift), value, 0.0)
    target[:, pl.ds(after, N)] += jnp.where(rows & (lane < shift), value, 0.0)


def paste_kernel(offsets, before, same, other, prev_same, prev_other, out, total, sems):
    core = here()[2]
    copies = []
    total[...] = jnp.zeros(total.shape, F32)
    for layer in range(PER_DEVICE):
        for part in range(2):
            target = total.at[layer, part]
            paste(offsets, core, same[layer, part], target, False)
            paste(offsets, 1 - core, other[layer, part], target, False)
            paste(before, core, prev_same[layer, part], target, True)
            paste(before, 1 - core, prev_other[layer, part], target, True)
            copy = pltpu.make_async_copy(target, out.at[layer, part], sems.at[layer, part])
            copy.start()
            copies.append(copy)
    for copy in copies:
        copy.wait()


def paste_windows(offsets, before, pieces, shape):
    return pl.pallas_call(
        paste_kernel,
        out_shape=jax.ShapeDtypeStruct(shape, F32),
        in_specs=[SMEM_SPEC] * 2 + [VMEM_SPEC] * 4,
        out_specs=ANY_SPEC,
        scratch_shapes=[pltpu.VMEM(shape, F32), pltpu.SemaphoreType.DMA((PER_DEVICE, 2))],
        name="paste_windows",
        compiler_params=PARAMS,
    )(offsets, before, *pieces)


def steps(first, count, change, windows, trail, twiddle, stages):
    def one(step, unused):
        layer = first + change * step
        slot = layer if change > 0 else layer + 1
        mixed = times(trail[slot, 0], trail[slot, 1], windows[layer, 0], windows[layer, 1])
        advance(*mixed, trail.at[slot + change], twiddle, stages)
        return unused

    lax.fori_loop(0, count, one, 0)


def keep(chip, trail, saved):
    for slot in range(PER_CHIP):
        saved[slot] = trail[chip * PER_CHIP + slot]


def first_kernel(near0, near1, up0, up1, far0, far1, down0, down1, wave, twiddle, *rest):
    leaving, saved, windows, trail, stages = rest
    stage, chip, core = here()
    sources = ((near0, near1), (up0, up1), (far0, far1), (down0, down1))

    @pl.when(stage == 0)
    def _():
        trail[0] = wave[...]

        def one_core(step, unused):
            owner, owner_core = step // CORES, step % CORES
            slot = (owner_core + core) % CORES
            for distance in range(RING):

                @pl.when((owner - chip + RING) % RING == distance)
                def _():
                    for parity in range(PER_DEVICE):
                        layer = step * PER_DEVICE + parity
                        window = sources[distance][parity][slot]
                        windows[layer] = window
                        mixed = times(trail[layer, 0], trail[layer, 1], window[0], window[1])
                        advance(*mixed, trail.at[layer + 1], twiddle, stages)

            return unused

        lax.fori_loop(0, RING * CORES, one_core, 0)
        leaving[...] = trail[PER_STAGE]
        keep(chip, trail, saved)

    @pl.when(stage != 0)
    def _():
        for distance in range(RING):
            owner = (chip + distance) % RING
            for slot in range(CORES):
                owner_core = core if slot == 0 else 1 - core
                for parity in range(PER_DEVICE):
                    layer = owner * PER_CHIP + owner_core * PER_DEVICE + parity
                    windows[layer] = sources[distance][parity][slot]


def forward_kernel(section, windows, wave, saved_in, twiddle, leaving, saved, trail, stages):
    stage, chip, core = here()

    @pl.when(stage == section)
    def _():
        trail[0] = wave[...]
        steps(0, PER_STAGE, 1, windows, trail, twiddle, stages)
        leaving[...] = trail[PER_STAGE]
        keep(chip, trail, saved)

    @pl.when(stage != section)
    def _():
        saved[...] = saved_in[...]


def gradients(chip, core, trail, psi_of, chirp, same, other):
    factor = squared(chirp)
    for slot in range(PER_CHIP):
        mine = slot < PER_DEVICE
        local = (core if mine else 1 - core) * PER_DEVICE + slot % PER_DEVICE
        layer = chip * PER_CHIP + local
        psi_re, psi_im = psi_of(layer, local)
        value = times(trail[layer + 1, 0], trail[layer + 1, 1], psi_re, psi_im)
        real, imag = times(*value, *factor)
        target = (same if mine else other).at[slot % PER_DEVICE]
        target[0] = (-real).T if slot % 2 else -real
        target[1] = imag.T if slot % 2 else imag


def backward_kernel(section, windows, wave, saved, twiddle, chirp, same_in, other_in, *rest):
    leaving, same, other, trail, stages = rest
    stage, chip, core = here()

    @pl.when(stage == section)
    def _():
        trail[PER_STAGE] = wave[...]
        last = PER_STAGE - 1
        steps(last, PER_STAGE, -1, windows, trail, twiddle, stages)
        leaving[...] = trail[0]
        gradients(
            chip,
            core,
            trail,
            lambda layer, local: (saved[local, 0], saved[local, 1]),
            chirp,
            same,
            other,
        )

    @pl.when(stage != section)
    def _():
        same[...] = same_in[...]
        other[...] = other_in[...]


def last_backward_kernel(windows, wave, saved, twiddle, chirp, same_in, other_in, *rest):
    same, other, trail, stages = rest
    stage, chip, core = here()

    @pl.when(stage == 0)
    def _():
        trail[PER_STAGE] = wave[...]
        last = PER_STAGE - 1
        steps(last, last, -1, windows, trail, twiddle, stages)
        gradients(
            chip,
            core,
            trail,
            lambda layer, local: (saved[local, 0], saved[local, 1]),
            chirp,
            same,
            other,
        )

    @pl.when(stage != 0)
    def _():
        same[...] = same_in[...]
        other[...] = other_in[...]


def turn_kernel(section, windows, wave, measured, twiddle, chirp, *rest):
    leaving, same, other, history, trail, stages = rest
    stage, chip, core = here()

    @pl.when(stage == section)
    def _():
        last = PER_STAGE - 1
        history[0] = wave[...]
        steps(0, last, 1, windows, history, twiddle, stages)
        mixed = times(history[last, 0], history[last, 1], windows[last, 0], windows[last, 1])
        mixed = times(*mixed, chirp[0], chirp[1])
        advance(*mixed, history.at[PER_STAGE], twiddle, stages)
        real, imag = history[PER_STAGE, 0], history[PER_STAGE, 1]
        misfit = real * real + imag * imag - measured[...]
        target = trail.at[PER_STAGE]
        advance(misfit * real, -(misfit * imag), target, twiddle, stages)
        real, imag = times(target[0], target[1], chirp[0], chirp[1])
        target[0] = imag * (-1.0 / N)
        target[1] = real * (1.0 / N)
        steps(last, PER_STAGE, -1, windows, trail, twiddle, stages)
        leaving[...] = trail[0]
        gradients(
            chip,
            core,
            trail,
            lambda layer, local: (history[layer, 0], history[layer, 1]),
            chirp,
            same,
            other,
        )


def first_stage(sources, wave, twiddle):
    return pl.pallas_call(
        first_kernel,
        out_shape=(WAVE, SAVED, STACK),
        in_specs=[VMEM_SPEC] * 10,
        scratch_shapes=[TRAIL, ROW_STAGES],
        name="first_stage",
        compiler_params=PARAMS,
    )(*sources, wave, twiddle)


def forward_stage(section, windows, wave, saved, twiddle):
    return pl.pallas_call(
        functools.partial(forward_kernel, section),
        out_shape=(WAVE, SAVED),
        scratch_shapes=[TRAIL, ROW_STAGES],
        name="forward_stage",
        compiler_params=PARAMS,
    )(windows, wave, saved, twiddle)


def backward_stage(section, *operands):
    last = section == 0
    return pl.pallas_call(
        last_backward_kernel if last else functools.partial(backward_kernel, section),
        out_shape=(PIECE, PIECE) if last else (WAVE, PIECE, PIECE),
        scratch_shapes=[TRAIL, ROW_STAGES],
        name="backward_stage",
        compiler_params=PARAMS,
    )(*operands)


def turn_stage(section, *operands):
    return pl.pallas_call(
        functools.partial(turn_kernel, section),
        out_shape=(WAVE, PIECE, PIECE),
        scratch_shapes=[TRAIL, TRAIL, ROW_STAGES],
        name="turn_stage",
        compiler_params=PARAMS,
    )(*operands)


def along_ring(value, steps):
    def target(device):
        stage, rest = divmod(device, RING * CORES)
        chip, core = divmod(rest, CORES)
        return (stage * RING + (chip + steps) % RING) * CORES + core

    pairs = [(device, target(device)) for device in range(STAGES * RING * CORES)]
    return lax.ppermute(value, "depth", pairs)


def along_stages(value, steps):
    count = STAGES * RING * CORES
    pairs = [(device, (device + steps * RING * CORES) % count) for device in range(count)]
    return lax.ppermute(value, "depth", pairs)


def across(value, strips, swap):
    rows, depth = lax.axis_size("pos"), lax.axis_size("depth")
    pairs = []
    for strip in range(rows):
        for device in range(depth):
            other = device ^ 1 if swap else device
            pairs.append((strip * depth + device, (strip + strips) % rows * depth + other))
    return lax.ppermute(value, ("pos", "depth"), pairs)


def body(object_field, offsets, probe, intensity, tables):
    twiddle, chirp = tables
    core = lax.axis_index("depth") % CORES
    rows = lax.axis_size("pos")
    padded = jnp.pad(offsets, ((0, PAD_ROWS - offsets.shape[0]), (0, N - offsets.shape[1])))
    before = lax.ppermute(padded, "pos", [(i, (i + 1) % rows) for i in range(rows)])
    before = before[:GROUP]

    own = cut_own(offsets, object_field, chirp, probe)
    own_same, wave, field = own[:2], own[3], own[4]
    own_other = across(own[2], 0, True)
    fore = cut_fore(before, field, own[5])
    fore_same = [across(fore[parity], -1, False) for parity in range(PER_DEVICE)]
    fore_other = [across(fore[2 + parity], -1, True) for parity in range(PER_DEVICE)]
    row_here = jnp.where(core == 0, offsets[0, 0], offsets[1, 0]) % N

    near, up, down = [], [], []
    index = jnp.arange(N, dtype=jnp.int32)
    for parity in range(PER_DEVICE):
        axis = (None, slice(None)) if parity else (slice(None), None)
        below = jnp.broadcast_to((index >= row_here)[axis], PLANE)
        near.append(
            jnp.stack(
                [
                    jnp.where(below, own_same[parity], fore_same[parity]),
                    jnp.where(below, own_other[parity], fore_other[parity]),
                ]
            )
        )
        up.append(along_ring(near[-1], -1))
        down.append(along_ring(near[-1], 1))
    far = [along_ring(up[0], -1), along_ring(down[1], 1)]

    wave, saved, windows = first_stage((*near, *up, *far, *down), wave, twiddle)
    for section in range(1, STAGES - 1):
        wave = along_stages(wave, 1)
        wave, saved = forward_stage(section, windows, wave, saved, twiddle)
    wave = along_stages(wave, 1)
    measured = lax.dynamic_index_in_dim(intensity, core, 0, keepdims=False)
    wave, same, other = turn_stage(STAGES - 1, windows, wave, measured, twiddle, chirp)
    for section in reversed(range(1, STAGES - 1)):
        wave = along_stages(wave, -1)
        wave, same, other = backward_stage(
            section, windows, wave, saved, twiddle, chirp, same, other
        )
    wave = along_stages(wave, -1)
    same, other = backward_stage(0, windows, wave, saved, twiddle, chirp, same, other)
    prev_same = across(same, 1, False)
    prev_other = across(other, 1, True)
    other, prev_same = lax.optimization_barrier((other, prev_same))
    own_other = across(other, 0, True)
    pieces = (same, own_other, prev_same, prev_other)
    return paste_windows(offsets, before, pieces, object_field.shape)


def solution(mesh):
    mapped = jax.shard_map(
        body,
        mesh=mesh,
        in_specs=(
            P("depth", None, "pos", None),
            P("pos", None),
            P(),
            P("pos", None, None),
            P(),
        ),
        out_specs=P("depth", None, "pos", None),
        check_vma=False,
    )
    tables = make_tables()

    def run(object_field, offsets, probe, intensity):
        constants = tuple(jnp.asarray(table) for table in tables)
        return mapped(object_field, offsets, probe, intensity, constants)

    return run
```

```python
import functools
import math

import jax
import jax.numpy as jnp
import numpy as np
from jax import lax
from jax.experimental import pallas as pl
from jax.experimental.pallas import tpu as pltpu
from jax.sharding import PartitionSpec as P

N = 128
CORES = 2
RING = 4
STAGES = 4
PER_DEVICE = 2
PER_CHIP = CORES * PER_DEVICE
PER_STAGE = RING * PER_CHIP
PLANE = (2, N, N)
F32 = jnp.float32
PARAMS = pltpu.CompilerParams(vmem_limit_bytes=20 << 20)
GROUP = 8
PITCH = GROUP + 1
TRAIL = pltpu.VMEM((PER_STAGE + 1,) + PLANE, F32)
ROW_STAGES = pltpu.VMEM((2, 2, 160, N), F32)
WAVE = jax.ShapeDtypeStruct(PLANE, F32)
PIECE = jax.ShapeDtypeStruct((PER_DEVICE,) + PLANE, F32)
SAVED = jax.ShapeDtypeStruct((PER_CHIP,) + PLANE, F32)
STACK = jax.ShapeDtypeStruct((PER_STAGE,) + PLANE, F32)
SMEM_SPEC = pl.BlockSpec(memory_space=pltpu.SMEM)
VMEM_SPEC = pl.BlockSpec(memory_space=pltpu.VMEM)
ANY_SPEC = pl.BlockSpec(memory_space=pl.ANY)


def make_tables():
    index = np.arange(N)
    turn = np.exp(1j * np.pi * (index * index % (2 * N)) / N)
    chirp = np.outer(turn, turn)
    first, second = np.divmod(index, GROUP)
    twiddle = np.exp(-2j * np.pi * first * second / N)[:, None] * np.ones((1, N))
    tables = (twiddle, np.conj(chirp))
    return tuple(np.stack([t.real, t.imag]).astype(np.float32) for t in tables)


def times(first_re, first_im, second_re, second_im):
    return (
        first_re * second_re - first_im * second_im,
        first_re * second_im + first_im * second_re,
    )


def rotate(value, numerator, count):
    real, imag = value
    if numerator == 0:
        return value
    if numerator * 4 == count:
        return imag, -real
    half = math.sqrt(0.5)
    if numerator * 8 == count:
        return (real + imag) * half, (imag - real) * half
    if numerator * 8 == 3 * count:
        return (imag - real) * half, -(real + imag) * half
    cosine = math.cos(2.0 * math.pi * numerator / count)
    sine = -math.sin(2.0 * math.pi * numerator / count)
    return real * cosine - imag * sine, real * sine + imag * cosine


def transform(values):
    count = len(values)
    if count == 1:
        return values
    even, odd = transform(values[0::2]), transform(values[1::2])
    result = [None] * count
    for k in range(count // 2):
        moved = rotate(odd[k], k, count)
        result[k] = (even[k][0] + moved[0], even[k][1] + moved[1])
        result[k + count // 2] = (even[k][0] - moved[0], even[k][1] - moved[1])
    return result


def transform_rows(real, imag, twiddle, stage, put):
    groups = [
        (real[GROUP * k : GROUP * (k + 1)], imag[GROUP * k : GROUP * (k + 1)])
        for k in range(N // GROUP)
    ]
    for k, value in enumerate(transform(groups)):
        rows = pl.ds(GROUP * k, GROUP)
        if k:
            value = times(*value, twiddle[0, rows], twiddle[1, rows])
        rows = pl.ds(PITCH * k, GROUP)
        stage[0, rows], stage[1, rows] = value
    for part in range(2):
        picked = [pl.ds(PITCH * GROUP * part + k, GROUP, stride=PITCH) for k in range(GROUP)]
        done = transform([(stage[0, rows], stage[1, rows]) for rows in picked])
        for k in range(GROUP):
            put(2 * k + part, done[k])


def advance(real, imag, target, twiddle, stages):
    rows = [None] * (N // GROUP)
    transform_rows(real, imag, twiddle, stages.at[0], rows.__setitem__)
    real, imag = (jnp.concatenate([row[k] for row in rows], axis=0).T for k in range(2))

    def put(k, value):
        place = pl.ds(GROUP * k, GROUP)
        target[0, place], target[1, place] = value

    transform_rows(real, imag, twiddle, stages.at[1], put)


def role(core, kind):
    flip = kind % 2
    number = jnp.where(core == flip, 0, 1)
    previous = number if kind < 2 else 1 - number
    return previous, number


def corner(offsets, before, core, kind):
    previous, number = role(core, kind)
    row = jnp.where(previous == 1, before[number, 0], offsets[number, 0]) % N
    column = jnp.where(previous == 1, before[number, 1], offsets[number, 1])
    tile = column // N
    after = pl.multiple_of(jnp.minimum(tile + 1, 3) * N, N)
    low = jnp.where(previous == 1, 0, row)
    high = jnp.where(previous == 1, row, N)
    return row, low, high, pl.multiple_of(tile * N, N), after, column % N


def squared(chirp):
    real, imag = chirp[0], chirp[1]
    return real * real - imag * imag, -2.0 * real * imag


def cut(place, field, chirp, targets):
    lane = lax.broadcasted_iota(jnp.int32, (N, N), 1)
    unused, unused, unused, tile, after, shift = place
    wrapped = lane < shift
    real, imag = squared(chirp)
    factor = (imag * (1.0 / N), real * (-1.0 / N))
    for layer in range(PER_DEVICE):
        value = [
            jnp.where(
                wrapped,
                field[layer, part, :, pl.ds(after, N)],
                field[layer, part, :, pl.ds(tile, N)],
            )
            for part in range(2)
        ]
        value = times(*value, *factor)
        for part in range(2):
            targets[layer, part] = value[part].T if layer % 2 else value[part]


def here():
    device = lax.axis_index("depth")
    return device // (CORES * RING), device // CORES % RING, device % CORES


def load_kernel(field, chirp, probe, field_out, chirp_out, probe_out):
    field_out[...] = field[...]
    chirp_out[...] = chirp[...]
    probe_out[...] = probe[...]


def cut_kernel(offsets, before, field, chirp, probe, same, other, moved_same, moved_other, wave):
    core = here()[2]
    for kind, target in ((2, moved_same), (3, moved_other), (0, same), (1, other)):
        cut(corner(offsets, before, core, kind), field, chirp, target)
    place = corner(offsets, before, core, 0)
    rolled = [pltpu.roll(pltpu.roll(probe[k], place[0], 0), place[5], 1) for k in range(2)]
    real, imag = times(*rolled, chirp[0], chirp[1])
    wave[0] = -imag
    wave[1] = real


def load(field, chirp, probe):
    return pl.pallas_call(
        load_kernel,
        out_shape=(jax.ShapeDtypeStruct(field.shape, F32), WAVE, WAVE),
        name="load",
        compiler_params=PARAMS,
    )(field, chirp, probe)


def cut_windows(offsets, before, field, chirp, probe):
    return pl.pallas_call(
        cut_kernel,
        out_shape=(PIECE,) * 4 + (WAVE,),
        in_specs=[SMEM_SPEC] * 2 + [VMEM_SPEC] * 3,
        name="cut_windows",
        compiler_params=PARAMS,
    )(offsets, before, field, chirp, probe)


def paste(place, value, target):
    row = lax.broadcasted_iota(jnp.int32, (N, N), 0)
    lane = lax.broadcasted_iota(jnp.int32, (N, N), 1)
    unused, low, high, tile, after, shift = place
    rows = (row >= low) & (row < high)
    target[:, pl.ds(tile, N)] += jnp.where(rows & (lane >= shift), value, 0.0)
    target[:, pl.ds(after, N)] += jnp.where(rows & (lane < shift), value, 0.0)


def paste_kernel(offsets, before, same, other, moved_same, moved_other, out, total, sems):
    core = here()[2]
    places = [corner(offsets, before, core, kind) for kind in range(4)]
    copies = []
    total[...] = jnp.zeros(total.shape, F32)
    for layer in range(PER_DEVICE):
        for part in range(2):
            target = total.at[layer, part]
            for place, source in zip(places, (same, other, moved_same, moved_other)):
                paste(place, source[layer, part], target)
            copy = pltpu.make_async_copy(target, out.at[layer, part], sems.at[layer, part])
            copy.start()
            copies.append(copy)
    for copy in copies:
        copy.wait()


def paste_windows(offsets, before, pieces, shape):
    return pl.pallas_call(
        paste_kernel,
        out_shape=jax.ShapeDtypeStruct(shape, F32),
        in_specs=[SMEM_SPEC] * 2 + [VMEM_SPEC] * 4,
        out_specs=ANY_SPEC,
        scratch_shapes=[pltpu.VMEM(shape, F32), pltpu.SemaphoreType.DMA((PER_DEVICE, 2))],
        name="paste_windows",
        compiler_params=PARAMS,
    )(offsets, before, *pieces)


def steps(first, count, change, windows, trail, twiddle, stages):
    def one(step, unused):
        layer = first + change * step
        slot = layer if change > 0 else layer + 1
        mixed = times(trail[slot, 0], trail[slot, 1], windows[layer, 0], windows[layer, 1])
        advance(*mixed, trail.at[slot + change], twiddle, stages)
        return unused

    lax.fori_loop(0, count, one, 0)


def keep(chip, trail, saved):
    for slot in range(PER_CHIP):
        saved[slot] = trail[chip * PER_CHIP + slot]


def first_kernel(near0, near1, up0, up1, far0, far1, down0, down1, wave, twiddle, *rest):
    leaving, saved, windows, trail, stages = rest
    stage, chip, core = here()
    sources = ((near0, near1), (up0, up1), (far0, far1), (down0, down1))

    @pl.when(stage == 0)
    def _():
        trail[0] = wave[...]

        def one_core(step, unused):
            owner, owner_core = step // CORES, step % CORES
            slot = (owner_core + core) % CORES
            for distance in range(RING):

                @pl.when((owner - chip + RING) % RING == distance)
                def _():
                    for parity in range(PER_DEVICE):
                        layer = step * PER_DEVICE + parity
                        window = sources[distance][parity][slot]
                        windows[layer] = window
                        mixed = times(trail[layer, 0], trail[layer, 1], window[0], window[1])
                        advance(*mixed, trail.at[layer + 1], twiddle, stages)

            return unused

        lax.fori_loop(0, RING * CORES, one_core, 0)
        leaving[...] = trail[PER_STAGE]
        keep(chip, trail, saved)

    @pl.when(stage != 0)
    def _():
        for distance in range(RING):
            owner = (chip + distance) % RING
            for slot in range(CORES):
                owner_core = core if slot == 0 else 1 - core
                for parity in range(PER_DEVICE):
                    layer = owner * PER_CHIP + owner_core * PER_DEVICE + parity
                    windows[layer] = sources[distance][parity][slot]


def forward_kernel(section, windows, wave, saved_in, twiddle, leaving, saved, trail, stages):
    stage, chip, core = here()

    @pl.when(stage == section)
    def _():
        trail[0] = wave[...]
        steps(0, PER_STAGE, 1, windows, trail, twiddle, stages)
        leaving[...] = trail[PER_STAGE]
        keep(chip, trail, saved)

    @pl.when(stage != section)
    def _():
        saved[...] = saved_in[...]


def gradients(chip, core, trail, psi_of, chirp, same, other):
    factor = squared(chirp)
    for slot in range(PER_CHIP):
        mine = slot < PER_DEVICE
        local = (core if mine else 1 - core) * PER_DEVICE + slot % PER_DEVICE
        layer = chip * PER_CHIP + local
        psi_re, psi_im = psi_of(layer, local)
        value = times(trail[layer + 1, 0], trail[layer + 1, 1], psi_re, psi_im)
        real, imag = times(*value, *factor)
        target = (same if mine else other).at[slot % PER_DEVICE]
        target[0] = (-real).T if slot % 2 else -real
        target[1] = imag.T if slot % 2 else imag


def backward_kernel(section, windows, wave, saved, twiddle, chirp, same_in, other_in, *rest):
    leaving, same, other, trail, stages = rest
    stage, chip, core = here()

    @pl.when(stage == section)
    def _():
        trail[PER_STAGE] = wave[...]
        last = PER_STAGE - 1
        steps(last, PER_STAGE, -1, windows, trail, twiddle, stages)
        leaving[...] = trail[0]
        gradients(
            chip,
            core,
            trail,
            lambda layer, local: (saved[local, 0], saved[local, 1]),
            chirp,
            same,
            other,
        )

    @pl.when(stage != section)
    def _():
        same[...] = same_in[...]
        other[...] = other_in[...]


def last_backward_kernel(windows, wave, saved, twiddle, chirp, same_in, other_in, *rest):
    same, other, trail, stages = rest
    stage, chip, core = here()

    @pl.when(stage == 0)
    def _():
        trail[PER_STAGE] = wave[...]
        last = PER_STAGE - 1
        steps(last, last, -1, windows, trail, twiddle, stages)
        gradients(
            chip,
            core,
            trail,
            lambda layer, local: (saved[local, 0], saved[local, 1]),
            chirp,
            same,
            other,
        )

    @pl.when(stage != 0)
    def _():
        same[...] = same_in[...]
        other[...] = other_in[...]


def turn_kernel(section, windows, wave, measured, twiddle, chirp, *rest):
    leaving, same, other, history, trail, stages = rest
    stage, chip, core = here()

    @pl.when(stage == section)
    def _():
        last = PER_STAGE - 1
        history[0] = wave[...]
        steps(0, last, 1, windows, history, twiddle, stages)
        mixed = times(history[last, 0], history[last, 1], windows[last, 0], windows[last, 1])
        mixed = times(*mixed, chirp[0], chirp[1])
        advance(*mixed, history.at[PER_STAGE], twiddle, stages)
        real, imag = history[PER_STAGE, 0], history[PER_STAGE, 1]
        misfit = real * real + imag * imag - measured[...]
        target = trail.at[PER_STAGE]
        advance(misfit * real, -(misfit * imag), target, twiddle, stages)
        real, imag = times(target[0], target[1], chirp[0], chirp[1])
        target[0] = imag * (-1.0 / N)
        target[1] = real * (1.0 / N)
        steps(last, PER_STAGE, -1, windows, trail, twiddle, stages)
        leaving[...] = trail[0]
        gradients(
            chip,
            core,
            trail,
            lambda layer, local: (history[layer, 0], history[layer, 1]),
            chirp,
            same,
            other,
        )


def first_stage(sources, wave, twiddle):
    return pl.pallas_call(
        first_kernel,
        out_shape=(WAVE, SAVED, STACK),
        in_specs=[VMEM_SPEC] * 10,
        scratch_shapes=[TRAIL, ROW_STAGES],
        name="first_stage",
        compiler_params=PARAMS,
    )(*sources, wave, twiddle)


def forward_stage(section, windows, wave, saved, twiddle):
    return pl.pallas_call(
        functools.partial(forward_kernel, section),
        out_shape=(WAVE, SAVED),
        scratch_shapes=[TRAIL, ROW_STAGES],
        name="forward_stage",
        compiler_params=PARAMS,
    )(windows, wave, saved, twiddle)


def backward_stage(section, *operands):
    last = section == 0
    return pl.pallas_call(
        last_backward_kernel if last else functools.partial(backward_kernel, section),
        out_shape=(PIECE, PIECE) if last else (WAVE, PIECE, PIECE),
        scratch_shapes=[TRAIL, ROW_STAGES],
        name="backward_stage",
        compiler_params=PARAMS,
    )(*operands)


def turn_stage(section, *operands):
    return pl.pallas_call(
        functools.partial(turn_kernel, section),
        out_shape=(WAVE, PIECE, PIECE),
        scratch_shapes=[TRAIL, TRAIL, ROW_STAGES],
        name="turn_stage",
        compiler_params=PARAMS,
    )(*operands)


def along_ring(value, steps):
    def target(device):
        stage, rest = divmod(device, RING * CORES)
        chip, core = divmod(rest, CORES)
        return (stage * RING + (chip + steps) % RING) * CORES + core

    pairs = [(device, target(device)) for device in range(STAGES * RING * CORES)]
    return lax.ppermute(value, "depth", pairs)


def along_stages(value, steps):
    count = STAGES * RING * CORES
    pairs = [(device, (device + steps * RING * CORES) % count) for device in range(count)]
    return lax.ppermute(value, "depth", pairs)


def swap_cores(value):
    depth = lax.axis_size("depth")
    return lax.ppermute(value, "depth", [(device, device ^ 1) for device in range(depth)])


def across(value, swap, outward):
    rows, depth = lax.axis_size("pos"), lax.axis_size("depth")
    pairs = []
    for strip in range(rows):
        for device in range(depth):
            core = device % CORES
            target = core ^ swap
            owner = core if outward else target
            step = (1 if owner == 0 else -1) * (1 if outward else -1)
            pairs.append(
                (strip * depth + device, (strip + step) % rows * depth + (device ^ swap))
            )
    return lax.ppermute(value, ("pos", "depth"), pairs)


def body(object_field, offsets, probe, intensity, tables):
    twiddle, chirp = tables
    core = lax.axis_index("depth") % CORES
    rows = lax.axis_size("pos")
    padding = ((0, GROUP - offsets.shape[0]), (0, N - offsets.shape[1]))
    message = jnp.concatenate([intensity[1], jnp.pad(offsets.astype(F32), padding)])
    message = lax.ppermute(message, "pos", [(i, (i + 1) % rows) for i in range(rows)])
    before = message[N:].astype(jnp.int32)
    measured = jnp.where(core == 0, intensity[0], message[:N])

    field, chirp_here, probe_here = load(object_field, chirp, probe)
    cuts = cut_windows(offsets, before, field, chirp_here, probe_here)
    same, other, moved_same, moved_other, wave = cuts
    moved_same = across(moved_same, 0, False)
    moved_other = across(moved_other, 1, False)
    other = swap_cores(other)

    row_here = jnp.where(core == 0, offsets[0, 0], before[1, 0]) % N
    low = jnp.where(core == 0, row_here, 0)
    high = jnp.where(core == 0, N, row_here)
    near, up, down = [], [], []
    index = jnp.arange(N, dtype=jnp.int32)
    inside = (index >= low) & (index < high)
    for parity in range(PER_DEVICE):
        axis = (None, slice(None)) if parity else (slice(None), None)
        here_rows = jnp.broadcast_to(inside[axis], PLANE)
        near.append(
            jnp.stack(
                [
                    jnp.where(here_rows, same[parity], moved_same[parity]),
                    jnp.where(here_rows, other[parity], moved_other[parity]),
                ]
            )
        )
        up.append(along_ring(near[-1], -1))
        down.append(along_ring(near[-1], 1))
    far = [along_ring(up[0], -1), along_ring(down[1], 1)]

    wave, saved, windows = first_stage((*near, *up, *far, *down), wave, twiddle)
    for section in range(1, STAGES - 1):
        wave = along_stages(wave, 1)
        wave, saved = forward_stage(section, windows, wave, saved, twiddle)
    wave = along_stages(wave, 1)
    wave, same, other = turn_stage(STAGES - 1, windows, wave, measured, twiddle, chirp)
    for section in reversed(range(1, STAGES - 1)):
        wave = along_stages(wave, -1)
        wave, same, other = backward_stage(
            section, windows, wave, saved, twiddle, chirp, same, other
        )
    wave = along_stages(wave, -1)
    same, other = backward_stage(0, windows, wave, saved, twiddle, chirp, same, other)
    moved_same = across(same, 0, True)
    moved_other = across(other, 1, True)
    other, moved_same = lax.optimization_barrier((other, moved_same))
    other = swap_cores(other)
    pieces = (same, other, moved_same, moved_other)
    return paste_windows(offsets, before, pieces, object_field.shape)


def solution(mesh):
    mapped = jax.shard_map(
        body,
        mesh=mesh,
        in_specs=(
            P("depth", None, "pos", None),
            P("pos", None),
            P(),
            P("pos", None, None),
            P(),
        ),
        out_specs=P("depth", None, "pos", None),
        check_vma=False,
    )
    tables = make_tables()

    def run(object_field, offsets, probe, intensity):
        constants = tuple(jnp.asarray(table) for table in tables)
        return mapped(object_field, offsets, probe, intensity, constants)

    return run
```

```python
import functools
import math

import jax
import jax.numpy as jnp
import numpy as np
from jax import lax
from jax.experimental import pallas as pl
from jax.experimental.pallas import tpu as pltpu
from jax.sharding import PartitionSpec as P

N = 128
CORES = 2
RING = 4
STAGES = 4
PER_DEVICE = 2
PER_CHIP = CORES * PER_DEVICE
PER_STAGE = RING * PER_CHIP
PLANE = (2, N, N)
F32 = jnp.float32
PARAMS = pltpu.CompilerParams(vmem_limit_bytes=20 << 20)
GROUP = 8
PITCH = N // GROUP + 1
TRAIL = pltpu.VMEM((PER_STAGE + 1,) + PLANE, F32)
ROW_STAGES = pltpu.VMEM((2, 2, 176, N), F32)
WAVE = jax.ShapeDtypeStruct(PLANE, F32)
PIECE = jax.ShapeDtypeStruct((PER_DEVICE,) + PLANE, F32)
SAVED = jax.ShapeDtypeStruct((PER_CHIP,) + PLANE, F32)
STACK = jax.ShapeDtypeStruct((PER_STAGE,) + PLANE, F32)
SMEM_SPEC = pl.BlockSpec(memory_space=pltpu.SMEM)
VMEM_SPEC = pl.BlockSpec(memory_space=pltpu.VMEM)
ANY_SPEC = pl.BlockSpec(memory_space=pl.ANY)


def make_tables():
    index = np.arange(N)
    turn = np.exp(1j * np.pi * (index * index % (2 * N)) / N)
    chirp = np.outer(turn, turn)
    first, second = np.divmod(index, N // GROUP)
    twiddle = np.exp(-2j * np.pi * first * second / N)[:, None] * np.ones((1, N))
    tables = (twiddle, np.conj(chirp))
    return tuple(np.stack([t.real, t.imag]).astype(np.float32) for t in tables)


def times(first_re, first_im, second_re, second_im):
    return (
        first_re * second_re - first_im * second_im,
        first_re * second_im + first_im * second_re,
    )


def rotate(value, numerator, count):
    real, imag = value
    if numerator == 0:
        return value
    if numerator * 4 == count:
        return imag, -real
    half = math.sqrt(0.5)
    if numerator * 8 == count:
        return (real + imag) * half, (imag - real) * half
    if numerator * 8 == 3 * count:
        return (imag - real) * half, -(real + imag) * half
    cosine = math.cos(2.0 * math.pi * numerator / count)
    sine = -math.sin(2.0 * math.pi * numerator / count)
    return real * cosine - imag * sine, real * sine + imag * cosine


def transform(values):
    count = len(values)
    if count == 1:
        return values
    even, odd = transform(values[0::2]), transform(values[1::2])
    result = [None] * count
    for k in range(count // 2):
        moved = rotate(odd[k], k, count)
        result[k] = (even[k][0] + moved[0], even[k][1] + moved[1])
        result[k + count // 2] = (even[k][0] - moved[0], even[k][1] - moved[1])
    return result


def transform_rows(real, imag, twiddle, stage, put):
    for part in range(2):
        blocks = []
        for k in range(GROUP):
            rows = slice(N // GROUP * k + GROUP * part, N // GROUP * k + GROUP * (part + 1))
            blocks.append((real[rows], imag[rows]))
        for k, value in enumerate(transform(blocks)):
            rows = pl.ds(N // GROUP * k + GROUP * part, GROUP)
            if k:
                value = times(*value, twiddle[0, rows], twiddle[1, rows])
            rows = pl.ds(PITCH * k + GROUP * part, GROUP)
            stage[0, rows], stage[1, rows] = value
    picked = [pl.ds(k, GROUP, stride=PITCH) for k in range(N // GROUP)]
    for k, value in enumerate(transform([(stage[0, rows], stage[1, rows]) for rows in picked])):
        put(k, value)


def advance(real, imag, target, twiddle, stages):
    rows = [None] * (N // GROUP)
    transform_rows(real, imag, twiddle, stages.at[0], rows.__setitem__)
    real, imag = (jnp.concatenate([row[k] for row in rows], axis=0).T for k in range(2))

    def put(k, value):
        place = pl.ds(GROUP * k, GROUP)
        target[0, place], target[1, place] = value

    transform_rows(real, imag, twiddle, stages.at[1], put)


def role(core, kind):
    flip = kind % 2
    number = jnp.where(core == flip, 0, 1)
    previous = number if kind < 2 else 1 - number
    return previous, number


def corner(corners, core, kind):
    previous, number = role(core, kind)
    line = 2 * previous + number
    row = corners[line, 0] % N
    column = corners[line, 1]
    tile = column // N
    after = pl.multiple_of(jnp.minimum(tile + 1, 3) * N, N)
    low = jnp.where(previous == 1, 0, row)
    high = jnp.where(previous == 1, row, N)
    return row, low, high, pl.multiple_of(tile * N, N), after, column % N


def squared(chirp):
    real, imag = chirp[0], chirp[1]
    return real * real - imag * imag, -2.0 * real * imag


def cut(place, field, chirp, targets):
    lane = lax.broadcasted_iota(jnp.int32, (N, N), 1)
    unused, unused, unused, tile, after, shift = place
    wrapped = lane < shift
    real, imag = squared(chirp)
    factor = (imag * (1.0 / N), real * (-1.0 / N))
    for layer in range(PER_DEVICE):
        value = [
            jnp.where(
                wrapped,
                field[layer, part, :, pl.ds(after, N)],
                field[layer, part, :, pl.ds(tile, N)],
            )
            for part in range(2)
        ]
        value = times(*value, *factor)
        for part in range(2):
            targets[layer, part] = value[part].T if layer % 2 else value[part]


def here():
    device = lax.axis_index("depth")
    return device // (CORES * RING), device // CORES % RING, device % CORES


def load_kernel(field, chirp, offsets, field_out, chirp_out, offsets_out):
    field_out[...] = field[...]
    chirp_out[...] = chirp[...]
    offsets_out[...] = offsets[...]


def wave_kernel(corners, chirp, probe, wave):
    place = corner(corners, here()[2], 0)
    rolled = [pltpu.roll(pltpu.roll(probe[k], place[0], 0), place[5], 1) for k in range(2)]
    real, imag = times(*rolled, chirp[0], chirp[1])
    wave[0] = -imag
    wave[1] = real


def cut_kernel(corners, field, chirp, same, other, moved_same, moved_other):
    core = here()[2]
    for kind, target in ((2, moved_same), (3, moved_other), (0, same), (1, other)):
        cut(corner(corners, core, kind), field, chirp, target)


def load(field, chirp, offsets):
    whole = jax.ShapeDtypeStruct(field.shape, F32)
    return pl.pallas_call(
        load_kernel,
        out_shape=(whole, WAVE, jax.ShapeDtypeStruct(offsets.shape, offsets.dtype)),
        name="load",
        compiler_params=PARAMS,
    )(field, chirp, offsets)


def cut_windows(corners, field, chirp):
    return pl.pallas_call(
        cut_kernel,
        out_shape=(PIECE,) * 4,
        in_specs=[SMEM_SPEC] + [VMEM_SPEC] * 2,
        name="cut_windows",
        compiler_params=PARAMS,
    )(corners, field, chirp)


def first_wave(corners, chirp, probe):
    return pl.pallas_call(
        wave_kernel,
        out_shape=WAVE,
        in_specs=[SMEM_SPEC] + [VMEM_SPEC] * 2,
        name="first_wave",
        compiler_params=PARAMS,
    )(corners, chirp, probe)


def paste(place, value, target):
    row = lax.broadcasted_iota(jnp.int32, (N, N), 0)
    lane = lax.broadcasted_iota(jnp.int32, (N, N), 1)
    unused, low, high, tile, after, shift = place
    rows = (row >= low) & (row < high)
    target[:, pl.ds(tile, N)] += jnp.where(rows & (lane >= shift), value, 0.0)
    target[:, pl.ds(after, N)] += jnp.where(rows & (lane < shift), value, 0.0)


def paste_kernel(corners, same, other, moved_same, moved_other, out, total, sems):
    core = here()[2]
    places = [corner(corners, core, kind) for kind in range(4)]
    copies = []
    total[...] = jnp.zeros(total.shape, F32)
    for layer in range(PER_DEVICE):
        for part in range(2):
            target = total.at[layer, part]
            for place, source in zip(places, (same, other, moved_same, moved_other)):
                paste(place, source[layer, part], target)
            copy = pltpu.make_async_copy(target, out.at[layer, part], sems.at[layer, part])
            copy.start()
            copies.append(copy)
    for copy in copies:
        copy.wait()


def paste_windows(corners, pieces, shape):
    return pl.pallas_call(
        paste_kernel,
        out_shape=jax.ShapeDtypeStruct(shape, F32),
        in_specs=[SMEM_SPEC] + [VMEM_SPEC] * 4,
        out_specs=ANY_SPEC,
        scratch_shapes=[pltpu.VMEM(shape, F32), pltpu.SemaphoreType.DMA((PER_DEVICE, 2))],
        name="paste_windows",
        compiler_params=PARAMS,
    )(corners, *pieces)


def steps(first, count, change, windows, trail, twiddle, stages):
    def one(step, unused):
        layer = first + change * step
        slot = layer if change > 0 else layer + 1
        mixed = times(trail[slot, 0], trail[slot, 1], windows[layer, 0], windows[layer, 1])
        advance(*mixed, trail.at[slot + change], twiddle, stages)
        return unused

    lax.fori_loop(0, count, one, 0)


def keep(chip, trail, saved):
    for slot in range(PER_CHIP):
        saved[slot] = trail[chip * PER_CHIP + slot]


def first_kernel(near0, near1, up0, up1, far0, far1, down0, down1, wave, twiddle, *rest):
    leaving, saved, windows, trail, stages = rest
    stage, chip, core = here()
    sources = ((near0, near1), (up0, up1), (far0, far1), (down0, down1))

    @pl.when(stage == 0)
    def _():
        trail[0] = wave[...]

        def one_core(step, unused):
            owner, owner_core = step // CORES, step % CORES
            slot = (owner_core + core) % CORES
            for distance in range(RING):

                @pl.when((owner - chip + RING) % RING == distance)
                def _():
                    for parity in range(PER_DEVICE):
                        layer = step * PER_DEVICE + parity
                        window = sources[distance][parity][slot]
                        windows[layer] = window
                        mixed = times(trail[layer, 0], trail[layer, 1], window[0], window[1])
                        advance(*mixed, trail.at[layer + 1], twiddle, stages)

            return unused

        lax.fori_loop(0, RING * CORES, one_core, 0)
        leaving[...] = trail[PER_STAGE]
        keep(chip, trail, saved)

    @pl.when(stage != 0)
    def _():
        for distance in range(RING):
            owner = (chip + distance) % RING
            for slot in range(CORES):
                owner_core = core if slot == 0 else 1 - core
                for parity in range(PER_DEVICE):
                    layer = owner * PER_CHIP + owner_core * PER_DEVICE + parity
                    windows[layer] = sources[distance][parity][slot]


def forward_kernel(section, windows, wave, saved_in, twiddle, leaving, saved, trail, stages):
    stage, chip, core = here()

    @pl.when(stage == section)
    def _():
        trail[0] = wave[...]
        steps(0, PER_STAGE, 1, windows, trail, twiddle, stages)
        leaving[...] = trail[PER_STAGE]
        keep(chip, trail, saved)

    @pl.when(stage != section)
    def _():
        saved[...] = saved_in[...]


def gradients(chip, core, trail, psi_of, chirp, same, other):
    factor = squared(chirp)
    for slot in range(PER_CHIP):
        mine = slot < PER_DEVICE
        local = (core if mine else 1 - core) * PER_DEVICE + slot % PER_DEVICE
        layer = chip * PER_CHIP + local
        psi_re, psi_im = psi_of(layer, local)
        value = times(trail[layer + 1, 0], trail[layer + 1, 1], psi_re, psi_im)
        real, imag = times(*value, *factor)
        target = (same if mine else other).at[slot % PER_DEVICE]
        target[0] = (-real).T if slot % 2 else -real
        target[1] = imag.T if slot % 2 else imag


def backward_kernel(section, windows, wave, saved, twiddle, chirp, same_in, other_in, *rest):
    leaving, same, other, trail, stages = rest
    stage, chip, core = here()

    @pl.when(stage == section)
    def _():
        trail[PER_STAGE] = wave[...]
        last = PER_STAGE - 1
        steps(last, PER_STAGE, -1, windows, trail, twiddle, stages)
        leaving[...] = trail[0]
        gradients(
            chip,
            core,
            trail,
            lambda layer, local: (saved[local, 0], saved[local, 1]),
            chirp,
            same,
            other,
        )

    @pl.when(stage != section)
    def _():
        same[...] = same_in[...]
        other[...] = other_in[...]


def last_backward_kernel(windows, wave, saved, twiddle, chirp, same_in, other_in, *rest):
    same, other, trail, stages = rest
    stage, chip, core = here()

    @pl.when(stage == 0)
    def _():
        trail[PER_STAGE] = wave[...]
        last = PER_STAGE - 1
        steps(last, last, -1, windows, trail, twiddle, stages)
        gradients(
            chip,
            core,
            trail,
            lambda layer, local: (saved[local, 0], saved[local, 1]),
            chirp,
            same,
            other,
        )

    @pl.when(stage != 0)
    def _():
        same[...] = same_in[...]
        other[...] = other_in[...]


def turn_kernel(section, windows, wave, measured, twiddle, chirp, *rest):
    leaving, same, other, history, trail, stages = rest
    stage, chip, core = here()

    @pl.when(stage == section)
    def _():
        last = PER_STAGE - 1
        history[0] = wave[...]
        steps(0, last, 1, windows, history, twiddle, stages)
        mixed = times(history[last, 0], history[last, 1], windows[last, 0], windows[last, 1])
        mixed = times(*mixed, chirp[0], chirp[1])
        advance(*mixed, history.at[PER_STAGE], twiddle, stages)
        real, imag = history[PER_STAGE, 0], history[PER_STAGE, 1]
        misfit = real * real + imag * imag - measured[...]
        target = trail.at[PER_STAGE]
        advance(misfit * real, -(misfit * imag), target, twiddle, stages)
        real, imag = times(target[0], target[1], chirp[0], chirp[1])
        target[0] = imag * (-1.0 / N)
        target[1] = real * (1.0 / N)
        steps(last, PER_STAGE, -1, windows, trail, twiddle, stages)
        leaving[...] = trail[0]
        gradients(
            chip,
            core,
            trail,
            lambda layer, local: (history[layer, 0], history[layer, 1]),
            chirp,
            same,
            other,
        )


def first_stage(sources, wave, twiddle):
    return pl.pallas_call(
        first_kernel,
        out_shape=(WAVE, SAVED, STACK),
        in_specs=[VMEM_SPEC] * 10,
        scratch_shapes=[TRAIL, ROW_STAGES],
        name="first_stage",
        compiler_params=PARAMS,
    )(*sources, wave, twiddle)


def forward_stage(section, windows, wave, saved, twiddle):
    return pl.pallas_call(
        functools.partial(forward_kernel, section),
        out_shape=(WAVE, SAVED),
        scratch_shapes=[TRAIL, ROW_STAGES],
        name="forward_stage",
        compiler_params=PARAMS,
    )(windows, wave, saved, twiddle)


def backward_stage(section, *operands):
    last = section == 0
    return pl.pallas_call(
        last_backward_kernel if last else functools.partial(backward_kernel, section),
        out_shape=(PIECE, PIECE) if last else (WAVE, PIECE, PIECE),
        scratch_shapes=[TRAIL, ROW_STAGES],
        name="backward_stage",
        compiler_params=PARAMS,
    )(*operands)


def turn_stage(section, *operands):
    return pl.pallas_call(
        functools.partial(turn_kernel, section),
        out_shape=(WAVE, PIECE, PIECE),
        scratch_shapes=[TRAIL, TRAIL, ROW_STAGES],
        name="turn_stage",
        compiler_params=PARAMS,
    )(*operands)


def along_ring(value, steps):
    def target(device):
        stage, rest = divmod(device, RING * CORES)
        chip, core = divmod(rest, CORES)
        return (stage * RING + (chip + steps) % RING) * CORES + core

    pairs = [(device, target(device)) for device in range(STAGES * RING * CORES)]
    return lax.ppermute(value, "depth", pairs)


def along_stages(value, steps):
    count = STAGES * RING * CORES
    pairs = [(device, (device + steps * RING * CORES) % count) for device in range(count)]
    return lax.ppermute(value, "depth", pairs)


def swap_cores(value):
    depth = lax.axis_size("depth")
    return lax.ppermute(value, "depth", [(device, device ^ 1) for device in range(depth)])


def across(value, swap, outward):
    rows, depth = lax.axis_size("pos"), lax.axis_size("depth")
    pairs = []
    for strip in range(rows):
        for device in range(depth):
            core = device % CORES
            target = core ^ swap
            owner = core if outward else target
            step = (1 if owner == 0 else -1) * (1 if outward else -1)
            pairs.append(
                (strip * depth + device, (strip + step) % rows * depth + (device ^ swap))
            )
    return lax.ppermute(value, ("pos", "depth"), pairs)


def body(object_field, offsets, probe, intensity, tables):
    twiddle, chirp = tables
    core = lax.axis_index("depth") % CORES
    rows = lax.axis_size("pos")
    onward = [(i, (i + 1) % rows) for i in range(rows)]
    intensity_before = lax.ppermute(intensity, "pos", onward)
    before = lax.ppermute(offsets, "pos", onward)
    before, intensity_before = lax.optimization_barrier((before, intensity_before))
    field, chirp_here, offsets = load(object_field, chirp, offsets)
    corners = jnp.concatenate([offsets, before])
    measured = jnp.where(core == 0, intensity[0], intensity_before[1])

    same, other, moved_same, moved_other = cut_windows(corners, field, chirp_here)
    moved_same = across(moved_same, 0, False)
    moved_other = across(moved_other, 1, False)
    other = swap_cores(other)

    row_here = jnp.where(core == 0, offsets[0, 0], before[1, 0]) % N
    low = jnp.where(core == 0, row_here, 0)
    high = jnp.where(core == 0, N, row_here)
    near, up, down = [], [], []
    index = jnp.arange(N, dtype=jnp.int32)
    inside = (index >= low) & (index < high)
    for parity in range(PER_DEVICE):
        axis = (None, slice(None)) if parity else (slice(None), None)
        here_rows = jnp.broadcast_to(inside[axis], PLANE)
        near.append(
            jnp.stack(
                [
                    jnp.where(here_rows, same[parity], moved_same[parity]),
                    jnp.where(here_rows, other[parity], moved_other[parity]),
                ]
            )
        )
        up.append(along_ring(near[-1], -1))
        down.append(along_ring(near[-1], 1))
    far = [along_ring(down[0], 1), along_ring(up[1], -1)]

    wave = first_wave(corners, chirp, probe)
    wave, saved, windows = first_stage((*near, *up, *far, *down), wave, twiddle)
    for section in range(1, STAGES - 1):
        wave = along_stages(wave, 1)
        wave, saved = forward_stage(section, windows, wave, saved, twiddle)
    wave = along_stages(wave, 1)
    wave, same, other = turn_stage(STAGES - 1, windows, wave, measured, twiddle, chirp)
    for section in reversed(range(1, STAGES - 1)):
        wave = along_stages(wave, -1)
        wave, same, other = backward_stage(
            section, windows, wave, saved, twiddle, chirp, same, other
        )
    wave = along_stages(wave, -1)
    same, other = backward_stage(0, windows, wave, saved, twiddle, chirp, same, other)
    moved_same = across(same, 0, True)
    moved_other = across(other, 1, True)
    other = swap_cores(other)
    pieces = (same, other, moved_same, moved_other)
    return paste_windows(corners, pieces, object_field.shape)


def solution(mesh):
    mapped = jax.shard_map(
        body,
        mesh=mesh,
        in_specs=(
            P("depth", None, "pos", None),
            P("pos", None),
            P(),
            P("pos", None, None),
            P(),
        ),
        out_specs=P("depth", None, "pos", None),
        check_vma=False,
    )
    tables = make_tables()

    def run(object_field, offsets, probe, intensity):
        constants = tuple(jnp.asarray(table) for table in tables)
        return mapped(object_field, offsets, probe, intensity, constants)

    return run
```

```python
import functools
import math

import jax
import jax.numpy as jnp
import numpy as np
from jax import lax
from jax.experimental import pallas as pl
from jax.experimental.pallas import tpu as pltpu
from jax.sharding import PartitionSpec as P

N = 128
CORES = 2
RING = 4
STAGES = 4
PER_DEVICE = 2
PER_CHIP = CORES * PER_DEVICE
PER_STAGE = RING * PER_CHIP
PLANE = (2, N, N)
F32 = jnp.float32
PARAMS = pltpu.CompilerParams(vmem_limit_bytes=20 << 20)
GROUP = 8
PITCH = N // GROUP + 1
TRAIL = pltpu.VMEM((PER_STAGE + 1,) + PLANE, F32)
ROW_STAGES = pltpu.VMEM((2, 2, 176, N), F32)
WAVE = jax.ShapeDtypeStruct(PLANE, F32)
PIECE = jax.ShapeDtypeStruct((PER_DEVICE,) + PLANE, F32)
SAVED = jax.ShapeDtypeStruct((PER_CHIP,) + PLANE, F32)
STACK = jax.ShapeDtypeStruct((PER_STAGE,) + PLANE, F32)
SMEM_SPEC = pl.BlockSpec(memory_space=pltpu.SMEM)
VMEM_SPEC = pl.BlockSpec(memory_space=pltpu.VMEM)
ANY_SPEC = pl.BlockSpec(memory_space=pl.ANY)


def make_tables():
    index = np.arange(N)
    turn = np.exp(1j * np.pi * (index * index % (2 * N)) / N)
    chirp = np.outer(turn, turn)
    first, second = np.divmod(index, N // GROUP)
    twiddle = np.exp(-2j * np.pi * first * second / N)[:, None] * np.ones((1, N))
    tables = (twiddle, np.conj(chirp))
    return tuple(np.stack([t.real, t.imag]).astype(np.float32) for t in tables)


def times(first_re, first_im, second_re, second_im):
    return (
        first_re * second_re - first_im * second_im,
        first_re * second_im + first_im * second_re,
    )


def rotate(value, numerator, count):
    real, imag = value
    if numerator == 0:
        return value
    if numerator * 4 == count:
        return imag, -real
    half = math.sqrt(0.5)
    if numerator * 8 == count:
        return (real + imag) * half, (imag - real) * half
    if numerator * 8 == 3 * count:
        return (imag - real) * half, -(real + imag) * half
    cosine = math.cos(2.0 * math.pi * numerator / count)
    sine = -math.sin(2.0 * math.pi * numerator / count)
    return real * cosine - imag * sine, real * sine + imag * cosine


def transform(values):
    count = len(values)
    if count == 1:
        return values
    even, odd = transform(values[0::2]), transform(values[1::2])
    result = [None] * count
    for k in range(count // 2):
        moved = rotate(odd[k], k, count)
        result[k] = (even[k][0] + moved[0], even[k][1] + moved[1])
        result[k + count // 2] = (even[k][0] - moved[0], even[k][1] - moved[1])
    return result


def transform_rows(real, imag, twiddle, stage, put):
    for part in range(2):
        blocks = []
        for k in range(GROUP):
            rows = slice(N // GROUP * k + GROUP * part, N // GROUP * k + GROUP * (part + 1))
            blocks.append((real[rows], imag[rows]))
        for k, value in enumerate(transform(blocks)):
            rows = pl.ds(N // GROUP * k + GROUP * part, GROUP)
            if k:
                value = times(*value, twiddle[0, rows], twiddle[1, rows])
            rows = pl.ds(PITCH * k + GROUP * part, GROUP)
            stage[0, rows], stage[1, rows] = value
    picked = [pl.ds(k, GROUP, stride=PITCH) for k in range(N // GROUP)]
    for k, value in enumerate(transform([(stage[0, rows], stage[1, rows]) for rows in picked])):
        put(k, value)


def advance(real, imag, target, twiddle, stages):
    rows = [None] * (N // GROUP)
    transform_rows(real, imag, twiddle, stages.at[0], rows.__setitem__)
    real, imag = (jnp.concatenate([row[k] for row in rows], axis=0).T for k in range(2))

    def put(k, value):
        place = pl.ds(GROUP * k, GROUP)
        target[0, place], target[1, place] = value

    transform_rows(real, imag, twiddle, stages.at[1], put)


def role(core, kind):
    flip = kind % 2
    number = jnp.where(core == flip, 0, 1)
    previous = number if kind < 2 else 1 - number
    return previous, number


def corner(corners, core, kind):
    previous, number = role(core, kind)
    line = 2 * previous + number
    row = corners[line, 0] % N
    column = corners[line, 1]
    tile = column // N
    after = pl.multiple_of(jnp.minimum(tile + 1, 3) * N, N)
    low = jnp.where(previous == 1, 0, row)
    high = jnp.where(previous == 1, row, N)
    return row, low, high, pl.multiple_of(tile * N, N), after, column % N


def squared(chirp):
    real, imag = chirp[0], chirp[1]
    return real * real - imag * imag, -2.0 * real * imag


def cut(place, field, chirp, targets):
    lane = lax.broadcasted_iota(jnp.int32, (N, N), 1)
    unused, unused, unused, tile, after, shift = place
    wrapped = lane < shift
    real, imag = squared(chirp)
    factor = (imag * (1.0 / N), real * (-1.0 / N))
    for layer in range(PER_DEVICE):
        value = [
            jnp.where(
                wrapped,
                field[layer, part, :, pl.ds(after, N)],
                field[layer, part, :, pl.ds(tile, N)],
            )
            for part in range(2)
        ]
        value = times(*value, *factor)
        for part in range(2):
            targets[layer, part] = value[part].T if layer % 2 else value[part]


def here():
    device = lax.axis_index("depth")
    return device // (CORES * RING), device // CORES % RING, device % CORES


def load_kernel(field, chirp, offsets, field_out, chirp_out, offsets_out):
    field_out[...] = field[...]
    chirp_out[...] = chirp[...]
    offsets_out[...] = offsets[...]


def wave_kernel(corners, chirp, probe, wave):
    place = corner(corners, here()[2], 0)
    rolled = [pltpu.roll(pltpu.roll(probe[k], place[0], 0), place[5], 1) for k in range(2)]
    real, imag = times(*rolled, chirp[0], chirp[1])
    wave[0] = -imag
    wave[1] = real


def cut_kernel(corners, field, chirp, same, other, moved_same, moved_other):
    core = here()[2]
    for kind, target in ((2, moved_same), (3, moved_other), (0, same), (1, other)):
        cut(corner(corners, core, kind), field, chirp, target)


def load(field, chirp, offsets):
    whole = jax.ShapeDtypeStruct(field.shape, F32)
    return pl.pallas_call(
        load_kernel,
        out_shape=(whole, WAVE, jax.ShapeDtypeStruct(offsets.shape, offsets.dtype)),
        name="load",
        compiler_params=PARAMS,
    )(field, chirp, offsets)


def cut_windows(corners, field, chirp):
    return pl.pallas_call(
        cut_kernel,
        out_shape=(PIECE,) * 4,
        in_specs=[SMEM_SPEC] + [VMEM_SPEC] * 2,
        name="cut_windows",
        compiler_params=PARAMS,
    )(corners, field, chirp)


def first_wave(corners, chirp, probe):
    return pl.pallas_call(
        wave_kernel,
        out_shape=WAVE,
        in_specs=[SMEM_SPEC] + [VMEM_SPEC] * 2,
        name="first_wave",
        compiler_params=PARAMS,
    )(corners, chirp, probe)


def paste(place, value, target):
    row = lax.broadcasted_iota(jnp.int32, (N, N), 0)
    lane = lax.broadcasted_iota(jnp.int32, (N, N), 1)
    unused, low, high, tile, after, shift = place
    rows = (row >= low) & (row < high)
    target[:, pl.ds(tile, N)] += jnp.where(rows & (lane >= shift), value, 0.0)
    target[:, pl.ds(after, N)] += jnp.where(rows & (lane < shift), value, 0.0)


def paste_kernel(corners, same, other, moved_same, moved_other, out, total, sems):
    core = here()[2]
    places = [corner(corners, core, kind) for kind in range(4)]
    copies = []
    total[...] = jnp.zeros(total.shape, F32)
    for layer in range(PER_DEVICE):
        for part in range(2):
            target = total.at[layer, part]
            for place, source in zip(places, (same, other, moved_same, moved_other)):
                paste(place, source[layer, part], target)
            copy = pltpu.make_async_copy(target, out.at[layer, part], sems.at[layer, part])
            copy.start()
            copies.append(copy)
    for copy in copies:
        copy.wait()


def paste_windows(corners, pieces, shape):
    return pl.pallas_call(
        paste_kernel,
        out_shape=jax.ShapeDtypeStruct(shape, F32),
        in_specs=[SMEM_SPEC] + [VMEM_SPEC] * 4,
        out_specs=ANY_SPEC,
        scratch_shapes=[pltpu.VMEM(shape, F32), pltpu.SemaphoreType.DMA((PER_DEVICE, 2))],
        name="paste_windows",
        compiler_params=PARAMS,
    )(corners, *pieces)


def steps(first, count, change, windows, trail, twiddle, stages):
    def one(step, unused):
        layer = first + change * step
        slot = layer if change > 0 else layer + 1
        mixed = times(trail[slot, 0], trail[slot, 1], windows[layer, 0], windows[layer, 1])
        advance(*mixed, trail.at[slot + change], twiddle, stages)
        return unused

    lax.fori_loop(0, count, one, 0)


def keep(chip, trail, saved):
    for slot in range(PER_CHIP):
        saved[slot] = trail[chip * PER_CHIP + slot]


def first_kernel(near0, near1, up0, up1, far0, far1, down0, down1, wave, twiddle, *rest):
    leaving, saved, windows, trail, stages = rest
    stage, chip, core = here()
    sources = ((near0, near1), (up0, up1), (far0, far1), (down0, down1))

    @pl.when(stage == 0)
    def _():
        trail[0] = wave[...]

        def one_core(step, unused):
            owner, owner_core = step // CORES, step % CORES
            slot = (owner_core + core) % CORES
            for distance in range(RING):

                @pl.when((owner - chip + RING) % RING == distance)
                def _():
                    for parity in range(PER_DEVICE):
                        layer = step * PER_DEVICE + parity
                        window = sources[distance][parity][slot]
                        windows[layer] = window
                        mixed = times(trail[layer, 0], trail[layer, 1], window[0], window[1])
                        advance(*mixed, trail.at[layer + 1], twiddle, stages)

            return unused

        lax.fori_loop(0, RING * CORES, one_core, 0)
        leaving[...] = trail[PER_STAGE]
        keep(chip, trail, saved)

    @pl.when(stage != 0)
    def _():
        for distance in range(RING):
            owner = (chip + distance) % RING
            for slot in range(CORES):
                owner_core = core if slot == 0 else 1 - core
                for parity in range(PER_DEVICE):
                    layer = owner * PER_CHIP + owner_core * PER_DEVICE + parity
                    windows[layer] = sources[distance][parity][slot]


def forward_kernel(section, windows, wave, saved_in, twiddle, leaving, saved, trail, stages):
    stage, chip, core = here()

    @pl.when(stage == section)
    def _():
        trail[0] = wave[...]
        steps(0, PER_STAGE, 1, windows, trail, twiddle, stages)
        leaving[...] = trail[PER_STAGE]
        keep(chip, trail, saved)

    @pl.when(stage != section)
    def _():
        saved[...] = saved_in[...]


def gradients(chip, core, trail, psi_of, chirp, same, other):
    factor = squared(chirp)
    for slot in range(PER_CHIP):
        mine = slot < PER_DEVICE
        local = (core if mine else 1 - core) * PER_DEVICE + slot % PER_DEVICE
        layer = chip * PER_CHIP + local
        psi_re, psi_im = psi_of(layer, local)
        value = times(trail[layer + 1, 0], trail[layer + 1, 1], psi_re, psi_im)
        real, imag = times(*value, *factor)
        target = (same if mine else other).at[slot % PER_DEVICE]
        target[0] = (-real).T if slot % 2 else -real
        target[1] = imag.T if slot % 2 else imag


def backward_kernel(section, windows, wave, saved, twiddle, chirp, same_in, other_in, *rest):
    leaving, same, other, trail, stages = rest
    stage, chip, core = here()

    @pl.when(stage == section)
    def _():
        trail[PER_STAGE] = wave[...]
        last = PER_STAGE - 1
        steps(last, PER_STAGE, -1, windows, trail, twiddle, stages)
        leaving[...] = trail[0]
        gradients(
            chip,
            core,
            trail,
            lambda layer, local: (saved[local, 0], saved[local, 1]),
            chirp,
            same,
            other,
        )

    @pl.when(stage != section)
    def _():
        same[...] = same_in[...]
        other[...] = other_in[...]


def last_backward_kernel(windows, wave, saved, twiddle, chirp, same_in, other_in, *rest):
    same, other, trail, stages = rest
    stage, chip, core = here()

    @pl.when(stage == 0)
    def _():
        trail[PER_STAGE] = wave[...]
        last = PER_STAGE - 1
        steps(last, last, -1, windows, trail, twiddle, stages)
        gradients(
            chip,
            core,
            trail,
            lambda layer, local: (saved[local, 0], saved[local, 1]),
            chirp,
            same,
            other,
        )

    @pl.when(stage != 0)
    def _():
        same[...] = same_in[...]
        other[...] = other_in[...]


def turn_kernel(section, windows, wave, measured, twiddle, chirp, *rest):
    leaving, same, other, history, trail, stages = rest
    stage, chip, core = here()

    @pl.when(stage == section)
    def _():
        last = PER_STAGE - 1
        history[0] = wave[...]
        steps(0, last, 1, windows, history, twiddle, stages)
        mixed = times(history[last, 0], history[last, 1], windows[last, 0], windows[last, 1])
        mixed = times(*mixed, chirp[0], chirp[1])
        advance(*mixed, history.at[PER_STAGE], twiddle, stages)
        real, imag = history[PER_STAGE, 0], history[PER_STAGE, 1]
        misfit = real * real + imag * imag - measured[...]
        target = trail.at[PER_STAGE]
        advance(misfit * real, -(misfit * imag), target, twiddle, stages)
        real, imag = times(target[0], target[1], chirp[0], chirp[1])
        target[0] = imag * (-1.0 / N)
        target[1] = real * (1.0 / N)
        steps(last, PER_STAGE, -1, windows, trail, twiddle, stages)
        leaving[...] = trail[0]
        gradients(
            chip,
            core,
            trail,
            lambda layer, local: (history[layer, 0], history[layer, 1]),
            chirp,
            same,
            other,
        )


def first_stage(sources, wave, twiddle):
    return pl.pallas_call(
        first_kernel,
        out_shape=(WAVE, SAVED, STACK),
        in_specs=[VMEM_SPEC] * 10,
        scratch_shapes=[TRAIL, ROW_STAGES],
        name="first_stage",
        compiler_params=PARAMS,
    )(*sources, wave, twiddle)


def forward_stage(section, windows, wave, saved, twiddle):
    return pl.pallas_call(
        functools.partial(forward_kernel, section),
        out_shape=(WAVE, SAVED),
        scratch_shapes=[TRAIL, ROW_STAGES],
        name="forward_stage",
        compiler_params=PARAMS,
    )(windows, wave, saved, twiddle)


def backward_stage(section, *operands):
    last = section == 0
    return pl.pallas_call(
        last_backward_kernel if last else functools.partial(backward_kernel, section),
        out_shape=(PIECE, PIECE) if last else (WAVE, PIECE, PIECE),
        scratch_shapes=[TRAIL, ROW_STAGES],
        name="backward_stage",
        compiler_params=PARAMS,
    )(*operands)


def turn_stage(section, *operands):
    return pl.pallas_call(
        functools.partial(turn_kernel, section),
        out_shape=(WAVE, PIECE, PIECE),
        scratch_shapes=[TRAIL, TRAIL, ROW_STAGES],
        name="turn_stage",
        compiler_params=PARAMS,
    )(*operands)


def along_ring(value, steps):
    def target(device):
        stage, rest = divmod(device, RING * CORES)
        chip, core = divmod(rest, CORES)
        return (stage * RING + (chip + steps) % RING) * CORES + core

    pairs = [(device, target(device)) for device in range(STAGES * RING * CORES)]
    return lax.ppermute(value, "depth", pairs)


def along_stages(value, steps):
    count = STAGES * RING * CORES
    pairs = [(device, (device + steps * RING * CORES) % count) for device in range(count)]
    return lax.ppermute(value, "depth", pairs)


def swap_cores(value):
    depth = lax.axis_size("depth")
    return lax.ppermute(value, "depth", [(device, device ^ 1) for device in range(depth)])


def across(value, swap, outward):
    rows, depth = lax.axis_size("pos"), lax.axis_size("depth")
    pairs = []
    for strip in range(rows):
        for device in range(depth):
            core = device % CORES
            target = core ^ swap
            owner = core if outward else target
            step = (1 if owner == 0 else -1) * (1 if outward else -1)
            pairs.append(
                (strip * depth + device, (strip + step) % rows * depth + (device ^ swap))
            )
    return lax.ppermute(value, ("pos", "depth"), pairs)


def body(object_field, offsets, probe, intensity, tables):
    twiddle, chirp = tables
    core = lax.axis_index("depth") % CORES
    rows = lax.axis_size("pos")
    onward = [(i, (i + 1) % rows) for i in range(rows)]
    padded = jnp.pad(offsets, ((0, N - offsets.shape[0]), (0, N - offsets.shape[1])))
    before = lax.ppermute(padded, "pos", onward)[: offsets.shape[0], : offsets.shape[1]]
    field, chirp_here, offsets = load(object_field, chirp, offsets)
    corners = jnp.concatenate([offsets, before])

    same, other, moved_same, moved_other = cut_windows(corners, field, chirp_here)
    moved_same = across(moved_same, 0, False)
    moved_other = across(moved_other, 1, False)
    other = swap_cores(other)

    row_here = jnp.where(core == 0, offsets[0, 0], before[1, 0]) % N
    low = jnp.where(core == 0, row_here, 0)
    high = jnp.where(core == 0, N, row_here)
    near, up, down = [], [], []
    index = jnp.arange(N, dtype=jnp.int32)
    inside = (index >= low) & (index < high)
    for parity in range(PER_DEVICE):
        axis = (None, slice(None)) if parity else (slice(None), None)
        here_rows = jnp.broadcast_to(inside[axis], PLANE)
        near.append(
            jnp.stack(
                [
                    jnp.where(here_rows, same[parity], moved_same[parity]),
                    jnp.where(here_rows, other[parity], moved_other[parity]),
                ]
            )
        )
        up.append(along_ring(near[-1], -1))
        down.append(along_ring(near[-1], 1))
    far = [along_ring(down[0], 1), along_ring(up[1], -1)]

    wave = first_wave(corners, chirp, probe)
    wave, saved, windows = first_stage((*near, *up, *far, *down), wave, twiddle)
    wave, intensity = lax.optimization_barrier((wave, intensity))
    intensity_before = lax.ppermute(intensity, "pos", onward)
    for section in range(1, STAGES - 1):
        wave = along_stages(wave, 1)
        wave, saved = forward_stage(section, windows, wave, saved, twiddle)
    wave = along_stages(wave, 1)
    measured = jnp.where(core == 0, intensity[0], intensity_before[1])
    wave, same, other = turn_stage(STAGES - 1, windows, wave, measured, twiddle, chirp)
    for section in reversed(range(1, STAGES - 1)):
        wave = along_stages(wave, -1)
        wave, same, other = backward_stage(
            section, windows, wave, saved, twiddle, chirp, same, other
        )
    wave = along_stages(wave, -1)
    same, other = backward_stage(0, windows, wave, saved, twiddle, chirp, same, other)
    moved_same = across(same, 0, True)
    moved_other = across(other, 1, True)
    other = swap_cores(other)
    pieces = (same, other, moved_same, moved_other)
    return paste_windows(corners, pieces, object_field.shape)


def solution(mesh):
    mapped = jax.shard_map(
        body,
        mesh=mesh,
        in_specs=(
            P("depth", None, "pos", None),
            P("pos", None),
            P(),
            P("pos", None, None),
            P(),
        ),
        out_specs=P("depth", None, "pos", None),
        check_vma=False,
    )
    tables = make_tables()

    def run(object_field, offsets, probe, intensity):
        constants = tuple(jnp.asarray(table) for table in tables)
        return mapped(object_field, offsets, probe, intensity, constants)

    return run
```

```python
import functools
import math

import jax
import jax.numpy as jnp
import numpy as np
from jax import lax
from jax.experimental import pallas as pl
from jax.experimental.pallas import tpu as pltpu
from jax.sharding import PartitionSpec as P

N = 128
CORES = 2
RING = 4
STAGES = 4
PER_DEVICE = 2
PER_CHIP = CORES * PER_DEVICE
PER_STAGE = RING * PER_CHIP
PLANE = (2, N, N)
F32 = jnp.float32
PARAMS = pltpu.CompilerParams(vmem_limit_bytes=20 << 20)
GROUP = 8
PITCH = N // GROUP + 1
TRAIL = pltpu.VMEM((PER_STAGE + 1,) + PLANE, F32)
ROW_STAGES = pltpu.VMEM((2, 2, 176, N), F32)
WAVE = jax.ShapeDtypeStruct(PLANE, F32)
PIECE = jax.ShapeDtypeStruct((PER_DEVICE,) + PLANE, F32)
SAVED = jax.ShapeDtypeStruct((PER_CHIP,) + PLANE, F32)
STACK = jax.ShapeDtypeStruct((PER_STAGE,) + PLANE, F32)
SMEM_SPEC = pl.BlockSpec(memory_space=pltpu.SMEM)
VMEM_SPEC = pl.BlockSpec(memory_space=pltpu.VMEM)
ANY_SPEC = pl.BlockSpec(memory_space=pl.ANY)


def make_tables():
    index = np.arange(N)
    turn = np.exp(1j * np.pi * (index * index % (2 * N)) / N)
    chirp = np.outer(turn, turn)
    first, second = np.divmod(index, N // GROUP)
    twiddle = np.exp(-2j * np.pi * first * second / N)[:, None] * np.ones((1, N))
    tables = (twiddle, np.conj(chirp))
    return tuple(np.stack([t.real, t.imag]).astype(np.float32) for t in tables)


def times(first_re, first_im, second_re, second_im):
    return (
        first_re * second_re - first_im * second_im,
        first_re * second_im + first_im * second_re,
    )


def rotate(value, numerator, count):
    real, imag = value
    if numerator == 0:
        return value
    if numerator * 4 == count:
        return imag, -real
    half = math.sqrt(0.5)
    if numerator * 8 == count:
        return (real + imag) * half, (imag - real) * half
    if numerator * 8 == 3 * count:
        return (imag - real) * half, -(real + imag) * half
    cosine = math.cos(2.0 * math.pi * numerator / count)
    sine = -math.sin(2.0 * math.pi * numerator / count)
    return real * cosine - imag * sine, real * sine + imag * cosine


def transform(values):
    count = len(values)
    if count == 1:
        return values
    even, odd = transform(values[0::2]), transform(values[1::2])
    result = [None] * count
    for k in range(count // 2):
        moved = rotate(odd[k], k, count)
        result[k] = (even[k][0] + moved[0], even[k][1] + moved[1])
        result[k + count // 2] = (even[k][0] - moved[0], even[k][1] - moved[1])
    return result


def transform_rows(real, imag, twiddle, stage, put):
    for part in range(2):
        blocks = []
        for k in range(GROUP):
            rows = slice(N // GROUP * k + GROUP * part, N // GROUP * k + GROUP * (part + 1))
            blocks.append((real[rows], imag[rows]))
        for k, value in enumerate(transform(blocks)):
            rows = pl.ds(N // GROUP * k + GROUP * part, GROUP)
            if k:
                value = times(*value, twiddle[0, rows], twiddle[1, rows])
            rows = pl.ds(PITCH * k + GROUP * part, GROUP)
            stage[0, rows], stage[1, rows] = value
    picked = [pl.ds(k, GROUP, stride=PITCH) for k in range(N // GROUP)]
    for k, value in enumerate(transform([(stage[0, rows], stage[1, rows]) for rows in picked])):
        put(k, value)


def advance(real, imag, target, twiddle, stages):
    rows = [None] * (N // GROUP)
    transform_rows(real, imag, twiddle, stages.at[0], rows.__setitem__)
    real, imag = (jnp.concatenate([row[k] for row in rows], axis=0).T for k in range(2))

    def put(k, value):
        place = pl.ds(GROUP * k, GROUP)
        target[0, place], target[1, place] = value

    transform_rows(real, imag, twiddle, stages.at[1], put)


def role(core, kind):
    flip = kind % 2
    number = jnp.where(core == flip, 0, 1)
    previous = number if kind < 2 else 1 - number
    return previous, number


def corner(corners, core, kind):
    previous, number = role(core, kind)
    line = 2 * previous + number
    row = corners[line, 0] % N
    column = corners[line, 1]
    tile = column // N
    after = pl.multiple_of(jnp.minimum(tile + 1, 3) * N, N)
    low = jnp.where(previous == 1, 0, row)
    high = jnp.where(previous == 1, row, N)
    return row, low, high, pl.multiple_of(tile * N, N), after, column % N


def squared(chirp):
    real, imag = chirp[0], chirp[1]
    return real * real - imag * imag, -2.0 * real * imag


def cut(place, field, chirp, targets):
    lane = lax.broadcasted_iota(jnp.int32, (N, N), 1)
    unused, unused, unused, tile, after, shift = place
    wrapped = lane < shift
    real, imag = squared(chirp)
    factor = (imag * (1.0 / N), real * (-1.0 / N))
    for layer in range(PER_DEVICE):
        value = [
            jnp.where(
                wrapped,
                field[layer, part, :, pl.ds(after, N)],
                field[layer, part, :, pl.ds(tile, N)],
            )
            for part in range(2)
        ]
        value = times(*value, *factor)
        for part in range(2):
            targets[layer, part] = value[part].T if layer % 2 else value[part]


def here():
    device = lax.axis_index("depth")
    return device // (CORES * RING), device // CORES % RING, device % CORES


def load_kernel(field, chirp, offsets, field_out, chirp_out, offsets_out):
    field_out[...] = field[...]
    chirp_out[...] = chirp[...]
    offsets_out[...] = offsets[...]


def wave_kernel(corners, chirp, probe, wave):
    place = corner(corners, here()[2], 0)
    rolled = [pltpu.roll(pltpu.roll(probe[k], place[0], 0), place[5], 1) for k in range(2)]
    real, imag = times(*rolled, chirp[0], chirp[1])
    wave[0] = -imag
    wave[1] = real


def cut_other_kernel(corners, field, chirp, other):
    cut(corner(corners, here()[2], 1), field, chirp, other)


def cut_kernel(corners, field, chirp, same, moved_same, moved_other):
    core = here()[2]
    for kind, target in ((2, moved_same), (3, moved_other), (0, same)):
        cut(corner(corners, core, kind), field, chirp, target)


def load(field, chirp, offsets):
    whole = jax.ShapeDtypeStruct(field.shape, F32)
    return pl.pallas_call(
        load_kernel,
        out_shape=(whole, WAVE, jax.ShapeDtypeStruct(offsets.shape, offsets.dtype)),
        name="load",
        compiler_params=PARAMS,
    )(field, chirp, offsets)


def cut_other(corners, field, chirp):
    return pl.pallas_call(
        cut_other_kernel,
        out_shape=PIECE,
        in_specs=[SMEM_SPEC] + [VMEM_SPEC] * 2,
        name="cut_other",
        compiler_params=PARAMS,
    )(corners, field, chirp)


def cut_windows(corners, field, chirp):
    return pl.pallas_call(
        cut_kernel,
        out_shape=(PIECE,) * 3,
        in_specs=[SMEM_SPEC] + [VMEM_SPEC] * 2,
        name="cut_windows",
        compiler_params=PARAMS,
    )(corners, field, chirp)


def first_wave(corners, chirp, probe):
    return pl.pallas_call(
        wave_kernel,
        out_shape=WAVE,
        in_specs=[SMEM_SPEC] + [VMEM_SPEC] * 2,
        name="first_wave",
        compiler_params=PARAMS,
    )(corners, chirp, probe)


def paste(place, value, target):
    row = lax.broadcasted_iota(jnp.int32, (N, N), 0)
    lane = lax.broadcasted_iota(jnp.int32, (N, N), 1)
    unused, low, high, tile, after, shift = place
    rows = (row >= low) & (row < high)
    target[:, pl.ds(tile, N)] += jnp.where(rows & (lane >= shift), value, 0.0)
    target[:, pl.ds(after, N)] += jnp.where(rows & (lane < shift), value, 0.0)


def paste_kernel(corners, same, other, moved_same, moved_other, out, total, sems):
    core = here()[2]
    places = [corner(corners, core, kind) for kind in range(4)]
    copies = []
    for layer in range(PER_DEVICE):
        for part in range(2):
            target = total.at[layer, part]
            target[...] = jnp.zeros(target.shape, F32)
            for place, source in zip(places, (same, other, moved_same, moved_other)):
                paste(place, source[layer, part], target)
            copy = pltpu.make_async_copy(target, out.at[layer, part], sems.at[layer, part])
            copy.start()
            copies.append(copy)
    for copy in copies:
        copy.wait()


def paste_windows(corners, pieces, shape):
    return pl.pallas_call(
        paste_kernel,
        out_shape=jax.ShapeDtypeStruct(shape, F32),
        in_specs=[SMEM_SPEC] + [VMEM_SPEC] * 4,
        out_specs=ANY_SPEC,
        scratch_shapes=[pltpu.VMEM(shape, F32), pltpu.SemaphoreType.DMA((PER_DEVICE, 2))],
        name="paste_windows",
        compiler_params=PARAMS,
    )(corners, *pieces)


def steps(first, count, change, windows, trail, twiddle, stages):
    def one(step, unused):
        layer = first + change * step
        slot = layer if change > 0 else layer + 1
        mixed = times(trail[slot, 0], trail[slot, 1], windows[layer, 0], windows[layer, 1])
        advance(*mixed, trail.at[slot + change], twiddle, stages)
        return unused

    lax.fori_loop(0, count, one, 0)


def keep(chip, trail, saved):
    for slot in range(PER_CHIP):
        saved[slot] = trail[chip * PER_CHIP + slot]


def first_kernel(near0, near1, up0, up1, far0, far1, down0, down1, wave, twiddle, *rest):
    leaving, saved, windows, trail, stages = rest
    stage, chip, core = here()
    sources = ((near0, near1), (up0, up1), (far0, far1), (down0, down1))

    @pl.when(stage == 0)
    def _():
        trail[0] = wave[...]

        def one_core(step, unused):
            owner, owner_core = step // CORES, step % CORES
            slot = (owner_core + core) % CORES
            for distance in range(RING):

                @pl.when((owner - chip + RING) % RING == distance)
                def _():
                    for parity in range(PER_DEVICE):
                        layer = step * PER_DEVICE + parity
                        window = sources[distance][parity][slot]
                        windows[layer] = window
                        mixed = times(trail[layer, 0], trail[layer, 1], window[0], window[1])
                        advance(*mixed, trail.at[layer + 1], twiddle, stages)

            return unused

        lax.fori_loop(0, RING * CORES, one_core, 0)
        leaving[...] = trail[PER_STAGE]
        keep(chip, trail, saved)

    @pl.when(stage != 0)
    def _():
        for distance in range(RING):
            owner = (chip + distance) % RING
            for slot in range(CORES):
                owner_core = core if slot == 0 else 1 - core
                for parity in range(PER_DEVICE):
                    layer = owner * PER_CHIP + owner_core * PER_DEVICE + parity
                    windows[layer] = sources[distance][parity][slot]


def forward_kernel(section, windows, wave, saved_in, twiddle, leaving, saved, trail, stages):
    stage, chip, core = here()

    @pl.when(stage == section)
    def _():
        trail[0] = wave[...]
        steps(0, PER_STAGE, 1, windows, trail, twiddle, stages)
        leaving[...] = trail[PER_STAGE]
        keep(chip, trail, saved)

    @pl.when(stage != section)
    def _():
        saved[...] = saved_in[...]


def gradients(chip, core, trail, psi_of, chirp, same, other):
    factor = squared(chirp)
    for slot in range(PER_CHIP):
        mine = slot < PER_DEVICE
        local = (core if mine else 1 - core) * PER_DEVICE + slot % PER_DEVICE
        layer = chip * PER_CHIP + local
        psi_re, psi_im = psi_of(layer, local)
        value = times(trail[layer + 1, 0], trail[layer + 1, 1], psi_re, psi_im)
        real, imag = times(*value, *factor)
        target = (same if mine else other).at[slot % PER_DEVICE]
        target[0] = (-real).T if slot % 2 else -real
        target[1] = imag.T if slot % 2 else imag


def backward_kernel(section, windows, wave, saved, twiddle, chirp, same_in, other_in, *rest):
    leaving, same, other, trail, stages = rest
    stage, chip, core = here()

    @pl.when(stage == section)
    def _():
        trail[PER_STAGE] = wave[...]
        last = PER_STAGE - 1
        steps(last, PER_STAGE, -1, windows, trail, twiddle, stages)
        leaving[...] = trail[0]
        gradients(
            chip,
            core,
            trail,
            lambda layer, local: (saved[local, 0], saved[local, 1]),
            chirp,
            same,
            other,
        )

    @pl.when(stage != section)
    def _():
        same[...] = same_in[...]
        other[...] = other_in[...]


def last_backward_kernel(windows, wave, saved, twiddle, chirp, same_in, other_in, *rest):
    same, other, trail, stages = rest
    stage, chip, core = here()

    @pl.when(stage == 0)
    def _():
        trail[PER_STAGE] = wave[...]
        last = PER_STAGE - 1
        steps(last, last, -1, windows, trail, twiddle, stages)
        gradients(
            chip,
            core,
            trail,
            lambda layer, local: (saved[local, 0], saved[local, 1]),
            chirp,
            same,
            other,
        )

    @pl.when(stage != 0)
    def _():
        same[...] = same_in[...]
        other[...] = other_in[...]


def turn_kernel(section, windows, wave, measured, twiddle, chirp, *rest):
    leaving, same, other, history, trail, stages = rest
    stage, chip, core = here()

    @pl.when(stage == section)
    def _():
        last = PER_STAGE - 1
        history[0] = wave[...]
        steps(0, last, 1, windows, history, twiddle, stages)
        mixed = times(history[last, 0], history[last, 1], windows[last, 0], windows[last, 1])
        mixed = times(*mixed, chirp[0], chirp[1])
        advance(*mixed, history.at[PER_STAGE], twiddle, stages)
        real, imag = history[PER_STAGE, 0], history[PER_STAGE, 1]
        misfit = real * real + imag * imag - measured[...]
        target = trail.at[PER_STAGE]
        advance(misfit * real, -(misfit * imag), target, twiddle, stages)
        real, imag = times(target[0], target[1], chirp[0], chirp[1])
        target[0] = imag * (-1.0 / N)
        target[1] = real * (1.0 / N)
        steps(last, PER_STAGE, -1, windows, trail, twiddle, stages)
        leaving[...] = trail[0]
        gradients(
            chip,
            core,
            trail,
            lambda layer, local: (history[layer, 0], history[layer, 1]),
            chirp,
            same,
            other,
        )


def first_stage(sources, wave, twiddle):
    return pl.pallas_call(
        first_kernel,
        out_shape=(WAVE, SAVED, STACK),
        in_specs=[VMEM_SPEC] * 10,
        scratch_shapes=[TRAIL, ROW_STAGES],
        name="first_stage",
        compiler_params=PARAMS,
    )(*sources, wave, twiddle)


def forward_stage(section, windows, wave, saved, twiddle):
    return pl.pallas_call(
        functools.partial(forward_kernel, section),
        out_shape=(WAVE, SAVED),
        scratch_shapes=[TRAIL, ROW_STAGES],
        name="forward_stage",
        compiler_params=PARAMS,
    )(windows, wave, saved, twiddle)


def backward_stage(section, *operands):
    last = section == 0
    return pl.pallas_call(
        last_backward_kernel if last else functools.partial(backward_kernel, section),
        out_shape=(PIECE, PIECE) if last else (WAVE, PIECE, PIECE),
        scratch_shapes=[TRAIL, ROW_STAGES],
        name="backward_stage",
        compiler_params=PARAMS,
    )(*operands)


def turn_stage(section, *operands):
    return pl.pallas_call(
        functools.partial(turn_kernel, section),
        out_shape=(WAVE, PIECE, PIECE),
        scratch_shapes=[TRAIL, TRAIL, ROW_STAGES],
        name="turn_stage",
        compiler_params=PARAMS,
    )(*operands)


def along_ring(value, steps):
    def target(device):
        stage, rest = divmod(device, RING * CORES)
        chip, core = divmod(rest, CORES)
        return (stage * RING + (chip + steps) % RING) * CORES + core

    pairs = [(device, target(device)) for device in range(STAGES * RING * CORES)]
    return lax.ppermute(value, "depth", pairs)


def along_stages(value, steps):
    count = STAGES * RING * CORES
    pairs = [(device, (device + steps * RING * CORES) % count) for device in range(count)]
    return lax.ppermute(value, "depth", pairs)


def swap_cores(value):
    depth = lax.axis_size("depth")
    return lax.ppermute(value, "depth", [(device, device ^ 1) for device in range(depth)])


def across(value, swap, outward):
    rows, depth = lax.axis_size("pos"), lax.axis_size("depth")
    pairs = []
    for strip in range(rows):
        for device in range(depth):
            core = device % CORES
            target = core ^ swap
            owner = core if outward else target
            step = (1 if owner == 0 else -1) * (1 if outward else -1)
            pairs.append(
                (strip * depth + device, (strip + step) % rows * depth + (device ^ swap))
            )
    return lax.ppermute(value, ("pos", "depth"), pairs)


def body(object_field, offsets, probe, intensity, tables):
    twiddle, chirp = tables
    core = lax.axis_index("depth") % CORES
    rows = lax.axis_size("pos")
    onward = [(i, (i + 1) % rows) for i in range(rows)]
    padded = jnp.pad(offsets, ((0, N - offsets.shape[0]), (0, N - offsets.shape[1])))
    before = lax.ppermute(padded, "pos", onward)[: offsets.shape[0], : offsets.shape[1]]
    field, chirp_here, offsets = load(object_field, chirp, offsets)
    corners = jnp.concatenate([offsets, before])

    other = cut_other(corners, field, chirp_here)
    same, moved_same, moved_other = cut_windows(corners, field, chirp_here)
    moved_same = across(moved_same, 0, False)
    moved_other = across(moved_other, 1, False)
    other = swap_cores(other)

    row_here = jnp.where(core == 0, offsets[0, 0], before[1, 0]) % N
    low = jnp.where(core == 0, row_here, 0)
    high = jnp.where(core == 0, N, row_here)
    near, up, down = [], [], []
    index = jnp.arange(N, dtype=jnp.int32)
    inside = (index >= low) & (index < high)
    for parity in range(PER_DEVICE):
        axis = (None, slice(None)) if parity else (slice(None), None)
        here_rows = jnp.broadcast_to(inside[axis], PLANE)
        near.append(
            jnp.stack(
                [
                    jnp.where(here_rows, same[parity], moved_same[parity]),
                    jnp.where(here_rows, other[parity], moved_other[parity]),
                ]
            )
        )
        up.append(along_ring(near[-1], -1))
        down.append(along_ring(near[-1], 1))
    far = [along_ring(down[0], 1), along_ring(up[1], -1)]

    wave = first_wave(corners, chirp, probe)
    wave, saved, windows = first_stage((*near, *up, *far, *down), wave, twiddle)
    wave, intensity = lax.optimization_barrier((wave, intensity))
    intensity_before = lax.ppermute(intensity, "pos", onward)
    for section in range(1, STAGES - 1):
        wave = along_stages(wave, 1)
        wave, saved = forward_stage(section, windows, wave, saved, twiddle)
    wave = along_stages(wave, 1)
    measured = jnp.where(core == 0, intensity[0], intensity_before[1])
    wave, same, other = turn_stage(STAGES - 1, windows, wave, measured, twiddle, chirp)
    for section in reversed(range(1, STAGES - 1)):
        wave = along_stages(wave, -1)
        wave, same, other = backward_stage(
            section, windows, wave, saved, twiddle, chirp, same, other
        )
    wave = along_stages(wave, -1)
    same, other = backward_stage(0, windows, wave, saved, twiddle, chirp, same, other)
    moved_same = across(same, 0, True)
    moved_other = across(other, 1, True)
    other = swap_cores(other)
    pieces = (same, other, moved_same, moved_other)
    return paste_windows(corners, pieces, object_field.shape)


def solution(mesh):
    mapped = jax.shard_map(
        body,
        mesh=mesh,
        in_specs=(
            P("depth", None, "pos", None),
            P("pos", None),
            P(),
            P("pos", None, None),
            P(),
        ),
        out_specs=P("depth", None, "pos", None),
        check_vma=False,
    )
    tables = make_tables()

    def run(object_field, offsets, probe, intensity):
        constants = tuple(jnp.asarray(table) for table in tables)
        return mapped(object_field, offsets, probe, intensity, constants)

    return run
```

```python
import functools
import math

import jax
import jax.numpy as jnp
import numpy as np
from jax import lax
from jax.experimental import pallas as pl
from jax.experimental.pallas import tpu as pltpu
from jax.sharding import PartitionSpec as P

N = 128
CORES = 2
RING = 4
STAGES = 4
PER_DEVICE = 2
PER_CHIP = CORES * PER_DEVICE
PER_STAGE = RING * PER_CHIP
PLANE = (2, N, N)
F32 = jnp.float32
PARAMS = pltpu.CompilerParams(vmem_limit_bytes=20 << 20)
GROUP = 8
PITCH = N // GROUP + 1
TRAIL = pltpu.VMEM((PER_STAGE + 1,) + PLANE, F32)
ROW_STAGES = pltpu.VMEM((2, 2, 176, N), F32)
WAVE = jax.ShapeDtypeStruct(PLANE, F32)
PIECE = jax.ShapeDtypeStruct((PER_DEVICE,) + PLANE, F32)
SAVED = jax.ShapeDtypeStruct((PER_CHIP,) + PLANE, F32)
STACK = jax.ShapeDtypeStruct((PER_STAGE,) + PLANE, F32)
SMEM_SPEC = pl.BlockSpec(memory_space=pltpu.SMEM)
VMEM_SPEC = pl.BlockSpec(memory_space=pltpu.VMEM)
ANY_SPEC = pl.BlockSpec(memory_space=pl.ANY)


def make_tables():
    index = np.arange(N)
    turn = np.exp(1j * np.pi * (index * index % (2 * N)) / N)
    chirp = np.outer(turn, turn)
    first, second = np.divmod(index, N // GROUP)
    twiddle = np.exp(-2j * np.pi * first * second / N)[:, None] * np.ones((1, N))
    tables = (twiddle, np.conj(chirp))
    return tuple(np.stack([t.real, t.imag]).astype(np.float32) for t in tables)


def times(first_re, first_im, second_re, second_im):
    return (
        first_re * second_re - first_im * second_im,
        first_re * second_im + first_im * second_re,
    )


def rotate(value, numerator, count):
    real, imag = value
    if numerator == 0:
        return value
    if numerator * 4 == count:
        return imag, -real
    half = math.sqrt(0.5)
    if numerator * 8 == count:
        return (real + imag) * half, (imag - real) * half
    if numerator * 8 == 3 * count:
        return (imag - real) * half, -(real + imag) * half
    cosine = math.cos(2.0 * math.pi * numerator / count)
    sine = -math.sin(2.0 * math.pi * numerator / count)
    return real * cosine - imag * sine, real * sine + imag * cosine


def transform(values):
    count = len(values)
    if count == 1:
        return values
    even, odd = transform(values[0::2]), transform(values[1::2])
    result = [None] * count
    for k in range(count // 2):
        moved = rotate(odd[k], k, count)
        result[k] = (even[k][0] + moved[0], even[k][1] + moved[1])
        result[k + count // 2] = (even[k][0] - moved[0], even[k][1] - moved[1])
    return result


def transform_rows(real, imag, twiddle, stage, put):
    for part in range(2):
        blocks = []
        for k in range(GROUP):
            rows = slice(N // GROUP * k + GROUP * part, N // GROUP * k + GROUP * (part + 1))
            blocks.append((real[rows], imag[rows]))
        for k, value in enumerate(transform(blocks)):
            rows = pl.ds(N // GROUP * k + GROUP * part, GROUP)
            if k:
                value = times(*value, twiddle[0, rows], twiddle[1, rows])
            rows = pl.ds(PITCH * k + GROUP * part, GROUP)
            stage[0, rows], stage[1, rows] = value
    picked = [pl.ds(k, GROUP, stride=PITCH) for k in range(N // GROUP)]
    for k, value in enumerate(transform([(stage[0, rows], stage[1, rows]) for rows in picked])):
        put(k, value)


def advance(real, imag, target, twiddle, stages):
    rows = [None] * (N // GROUP)
    transform_rows(real, imag, twiddle, stages.at[0], rows.__setitem__)
    real, imag = (jnp.concatenate([row[k] for row in rows], axis=0).T for k in range(2))

    def put(k, value):
        place = pl.ds(GROUP * k, GROUP)
        target[0, place], target[1, place] = value

    transform_rows(real, imag, twiddle, stages.at[1], put)


def role(core, kind):
    flip = kind % 2
    number = jnp.where(core == flip, 0, 1)
    previous = number if kind < 2 else 1 - number
    return previous, number


def corner(corners, core, kind):
    previous, number = role(core, kind)
    line = 2 * previous + number
    row = corners[line, 0] % N
    column = corners[line, 1]
    tile = column // N
    after = pl.multiple_of(jnp.minimum(tile + 1, 3) * N, N)
    low = jnp.where(previous == 1, 0, row)
    high = jnp.where(previous == 1, row, N)
    return row, low, high, pl.multiple_of(tile * N, N), after, column % N


def squared(chirp):
    real, imag = chirp[0], chirp[1]
    return real * real - imag * imag, -2.0 * real * imag


def cut(place, field, chirp, targets):
    lane = lax.broadcasted_iota(jnp.int32, (N, N), 1)
    unused, unused, unused, tile, after, shift = place
    wrapped = lane < shift
    real, imag = squared(chirp)
    factor = (imag * (1.0 / N), real * (-1.0 / N))
    for layer in range(PER_DEVICE):
        value = [
            jnp.where(
                wrapped,
                field[layer, part, :, pl.ds(after, N)],
                field[layer, part, :, pl.ds(tile, N)],
            )
            for part in range(2)
        ]
        value = times(*value, *factor)
        for part in range(2):
            targets[layer, part] = value[part].T if layer % 2 else value[part]


def here():
    device = lax.axis_index("depth")
    return device // (CORES * RING), device // CORES % RING, device % CORES


def load_kernel(field, chirp, offsets, field_out, chirp_out, offsets_out):
    field_out[...] = field[...]
    chirp_out[...] = chirp[...]
    offsets_out[...] = offsets[...]


def wave_kernel(corners, chirp, probe, wave):
    place = corner(corners, here()[2], 0)
    rolled = [pltpu.roll(pltpu.roll(probe[k], place[0], 0), place[5], 1) for k in range(2)]
    real, imag = times(*rolled, chirp[0], chirp[1])
    wave[0] = -imag
    wave[1] = real


def cut_other_kernel(corners, field, chirp, other):
    cut(corner(corners, here()[2], 1), field, chirp, other)


def cut_kernel(corners, field, chirp, same, moved_same, moved_other):
    core = here()[2]
    for kind, target in ((2, moved_same), (3, moved_other), (0, same)):
        cut(corner(corners, core, kind), field, chirp, target)


def load(field, chirp, offsets):
    whole = jax.ShapeDtypeStruct(field.shape, F32)
    return pl.pallas_call(
        load_kernel,
        out_shape=(whole, WAVE, jax.ShapeDtypeStruct(offsets.shape, offsets.dtype)),
        name="load",
        compiler_params=PARAMS,
    )(field, chirp, offsets)


def cut_other(corners, field, chirp):
    return pl.pallas_call(
        cut_other_kernel,
        out_shape=PIECE,
        in_specs=[SMEM_SPEC] + [VMEM_SPEC] * 2,
        name="cut_other",
        compiler_params=PARAMS,
    )(corners, field, chirp)


def cut_windows(corners, field, chirp):
    return pl.pallas_call(
        cut_kernel,
        out_shape=(PIECE,) * 3,
        in_specs=[SMEM_SPEC] + [VMEM_SPEC] * 2,
        name="cut_windows",
        compiler_params=PARAMS,
    )(corners, field, chirp)


def first_wave(corners, chirp, probe):
    return pl.pallas_call(
        wave_kernel,
        out_shape=WAVE,
        in_specs=[SMEM_SPEC] + [VMEM_SPEC] * 2,
        name="first_wave",
        compiler_params=PARAMS,
    )(corners, chirp, probe)


def paste(place, value, target):
    row = lax.broadcasted_iota(jnp.int32, (N, N), 0)
    lane = lax.broadcasted_iota(jnp.int32, (N, N), 1)
    unused, low, high, tile, after, shift = place
    rows = (row >= low) & (row < high)
    target[:, pl.ds(tile, N)] += jnp.where(rows & (lane >= shift), value, 0.0)
    target[:, pl.ds(after, N)] += jnp.where(rows & (lane < shift), value, 0.0)


def paste_kernel(corners, same, other, moved_same, moved_other, out, total, sems):
    core = here()[2]
    places = [corner(corners, core, kind) for kind in range(4)]
    copies = []
    for layer in range(PER_DEVICE):
        for part in range(2):
            target = total.at[layer, part]
            target[...] = jnp.zeros(target.shape, F32)
            for place, source in zip(places, (same, other, moved_same, moved_other)):
                paste(place, source[layer, part], target)
            copy = pltpu.make_async_copy(target, out.at[layer, part], sems.at[layer, part])
            copy.start()
            copies.append(copy)
    for copy in copies:
        copy.wait()


def paste_windows(corners, pieces, shape):
    return pl.pallas_call(
        paste_kernel,
        out_shape=jax.ShapeDtypeStruct(shape, F32),
        in_specs=[SMEM_SPEC] + [VMEM_SPEC] * 4,
        out_specs=ANY_SPEC,
        scratch_shapes=[pltpu.VMEM(shape, F32), pltpu.SemaphoreType.DMA((PER_DEVICE, 2))],
        name="paste_windows",
        compiler_params=PARAMS,
    )(corners, *pieces)


def steps(first, count, change, windows, trail, twiddle, stages):
    def one(step, unused):
        layer = first + change * step
        slot = layer if change > 0 else layer + 1
        mixed = times(trail[slot, 0], trail[slot, 1], windows[layer, 0], windows[layer, 1])
        advance(*mixed, trail.at[slot + change], twiddle, stages)
        return unused

    lax.fori_loop(0, count, one, 0, unroll=2 if count % 2 == 0 else 3)


def keep(chip, trail, saved):
    for slot in range(PER_CHIP):
        saved[slot] = trail[chip * PER_CHIP + slot]


def first_kernel(near0, near1, up0, up1, far0, far1, down0, down1, wave, twiddle, *rest):
    leaving, saved, windows, trail, stages = rest
    stage, chip, core = here()
    sources = ((near0, near1), (up0, up1), (far0, far1), (down0, down1))

    @pl.when(stage == 0)
    def _():
        trail[0] = wave[...]

        def one_core(step, unused):
            owner, owner_core = step // CORES, step % CORES
            slot = (owner_core + core) % CORES
            for distance in range(RING):

                @pl.when((owner - chip + RING) % RING == distance)
                def _():
                    for parity in range(PER_DEVICE):
                        layer = step * PER_DEVICE + parity
                        window = sources[distance][parity][slot]
                        windows[layer] = window
                        mixed = times(trail[layer, 0], trail[layer, 1], window[0], window[1])
                        advance(*mixed, trail.at[layer + 1], twiddle, stages)

            return unused

        lax.fori_loop(0, RING * CORES, one_core, 0)
        leaving[...] = trail[PER_STAGE]
        keep(chip, trail, saved)

    @pl.when(stage != 0)
    def _():
        for distance in range(RING):
            owner = (chip + distance) % RING
            for slot in range(CORES):
                owner_core = core if slot == 0 else 1 - core
                for parity in range(PER_DEVICE):
                    layer = owner * PER_CHIP + owner_core * PER_DEVICE + parity
                    windows[layer] = sources[distance][parity][slot]


def forward_kernel(section, windows, wave, saved_in, twiddle, leaving, saved, trail, stages):
    stage, chip, core = here()

    @pl.when(stage == section)
    def _():
        trail[0] = wave[...]
        steps(0, PER_STAGE, 1, windows, trail, twiddle, stages)
        leaving[...] = trail[PER_STAGE]
        keep(chip, trail, saved)

    @pl.when(stage != section)
    def _():
        saved[...] = saved_in[...]


def gradients(chip, core, trail, psi_of, chirp, same, other):
    factor = squared(chirp)
    for slot in range(PER_CHIP):
        mine = slot < PER_DEVICE
        local = (core if mine else 1 - core) * PER_DEVICE + slot % PER_DEVICE
        layer = chip * PER_CHIP + local
        psi_re, psi_im = psi_of(layer, local)
        value = times(trail[layer + 1, 0], trail[layer + 1, 1], psi_re, psi_im)
        real, imag = times(*value, *factor)
        target = (same if mine else other).at[slot % PER_DEVICE]
        target[0] = (-real).T if slot % 2 else -real
        target[1] = imag.T if slot % 2 else imag


def backward_kernel(section, windows, wave, saved, twiddle, chirp, same_in, other_in, *rest):
    leaving, same, other, trail, stages = rest
    stage, chip, core = here()

    @pl.when(stage == section)
    def _():
        trail[PER_STAGE] = wave[...]
        last = PER_STAGE - 1
        steps(last, PER_STAGE, -1, windows, trail, twiddle, stages)
        leaving[...] = trail[0]
        gradients(
            chip,
            core,
            trail,
            lambda layer, local: (saved[local, 0], saved[local, 1]),
            chirp,
            same,
            other,
        )

    @pl.when(stage != section)
    def _():
        same[...] = same_in[...]
        other[...] = other_in[...]


def last_backward_kernel(windows, wave, saved, twiddle, chirp, same_in, other_in, *rest):
    same, other, trail, stages = rest
    stage, chip, core = here()

    @pl.when(stage == 0)
    def _():
        trail[PER_STAGE] = wave[...]
        last = PER_STAGE - 1
        steps(last, last, -1, windows, trail, twiddle, stages)
        gradients(
            chip,
            core,
            trail,
            lambda layer, local: (saved[local, 0], saved[local, 1]),
            chirp,
            same,
            other,
        )

    @pl.when(stage != 0)
    def _():
        same[...] = same_in[...]
        other[...] = other_in[...]


def turn_kernel(section, windows, wave, measured, twiddle, chirp, *rest):
    leaving, same, other, history, trail, stages = rest
    stage, chip, core = here()

    @pl.when(stage == section)
    def _():
        last = PER_STAGE - 1
        history[0] = wave[...]
        steps(0, last, 1, windows, history, twiddle, stages)
        mixed = times(history[last, 0], history[last, 1], windows[last, 0], windows[last, 1])
        mixed = times(*mixed, chirp[0], chirp[1])
        advance(*mixed, history.at[PER_STAGE], twiddle, stages)
        real, imag = history[PER_STAGE, 0], history[PER_STAGE, 1]
        misfit = real * real + imag * imag - measured[...]
        target = trail.at[PER_STAGE]
        advance(misfit * real, -(misfit * imag), target, twiddle, stages)
        real, imag = times(target[0], target[1], chirp[0], chirp[1])
        target[0] = imag * (-1.0 / N)
        target[1] = real * (1.0 / N)
        steps(last, PER_STAGE, -1, windows, trail, twiddle, stages)
        leaving[...] = trail[0]
        gradients(
            chip,
            core,
            trail,
            lambda layer, local: (history[layer, 0], history[layer, 1]),
            chirp,
            same,
            other,
        )


def first_stage(sources, wave, twiddle):
    return pl.pallas_call(
        first_kernel,
        out_shape=(WAVE, SAVED, STACK),
        in_specs=[VMEM_SPEC] * 10,
        scratch_shapes=[TRAIL, ROW_STAGES],
        name="first_stage",
        compiler_params=PARAMS,
    )(*sources, wave, twiddle)


def forward_stage(section, windows, wave, saved, twiddle):
    return pl.pallas_call(
        functools.partial(forward_kernel, section),
        out_shape=(WAVE, SAVED),
        scratch_shapes=[TRAIL, ROW_STAGES],
        name="forward_stage",
        compiler_params=PARAMS,
    )(windows, wave, saved, twiddle)


def backward_stage(section, *operands):
    last = section == 0
    return pl.pallas_call(
        last_backward_kernel if last else functools.partial(backward_kernel, section),
        out_shape=(PIECE, PIECE) if last else (WAVE, PIECE, PIECE),
        scratch_shapes=[TRAIL, ROW_STAGES],
        name="backward_stage",
        compiler_params=PARAMS,
    )(*operands)


def turn_stage(section, *operands):
    return pl.pallas_call(
        functools.partial(turn_kernel, section),
        out_shape=(WAVE, PIECE, PIECE),
        scratch_shapes=[TRAIL, TRAIL, ROW_STAGES],
        name="turn_stage",
        compiler_params=PARAMS,
    )(*operands)


def along_ring(value, steps):
    def target(device):
        stage, rest = divmod(device, RING * CORES)
        chip, core = divmod(rest, CORES)
        return (stage * RING + (chip + steps) % RING) * CORES + core

    pairs = [(device, target(device)) for device in range(STAGES * RING * CORES)]
    return lax.ppermute(value, "depth", pairs)


def along_stages(value, steps):
    count = STAGES * RING * CORES
    pairs = [(device, (device + steps * RING * CORES) % count) for device in range(count)]
    return lax.ppermute(value, "depth", pairs)


def swap_cores(value):
    depth = lax.axis_size("depth")
    return lax.ppermute(value, "depth", [(device, device ^ 1) for device in range(depth)])


def across(value, swap, outward):
    rows, depth = lax.axis_size("pos"), lax.axis_size("depth")
    pairs = []
    for strip in range(rows):
        for device in range(depth):
            core = device % CORES
            target = core ^ swap
            owner = core if outward else target
            step = (1 if owner == 0 else -1) * (1 if outward else -1)
            pairs.append(
                (strip * depth + device, (strip + step) % rows * depth + (device ^ swap))
            )
    return lax.ppermute(value, ("pos", "depth"), pairs)


def body(object_field, offsets, probe, intensity, tables):
    twiddle, chirp = tables
    core = lax.axis_index("depth") % CORES
    rows = lax.axis_size("pos")
    onward = [(i, (i + 1) % rows) for i in range(rows)]
    padded = jnp.pad(offsets, ((0, N - offsets.shape[0]), (0, N - offsets.shape[1])))
    before = lax.ppermute(padded, "pos", onward)[: offsets.shape[0], : offsets.shape[1]]
    field, chirp_here, offsets = load(object_field, chirp, offsets)
    corners = jnp.concatenate([offsets, before])

    other = cut_other(corners, field, chirp_here)
    same, moved_same, moved_other = cut_windows(corners, field, chirp_here)
    moved_same = across(moved_same, 0, False)
    moved_other = across(moved_other, 1, False)
    other = swap_cores(other)

    row_here = jnp.where(core == 0, offsets[0, 0], before[1, 0]) % N
    low = jnp.where(core == 0, row_here, 0)
    high = jnp.where(core == 0, N, row_here)
    near, up, down = [], [], []
    index = jnp.arange(N, dtype=jnp.int32)
    inside = (index >= low) & (index < high)
    for parity in range(PER_DEVICE):
        axis = (None, slice(None)) if parity else (slice(None), None)
        here_rows = jnp.broadcast_to(inside[axis], PLANE)
        near.append(
            jnp.stack(
                [
                    jnp.where(here_rows, same[parity], moved_same[parity]),
                    jnp.where(here_rows, other[parity], moved_other[parity]),
                ]
            )
        )
        up.append(along_ring(near[-1], -1))
        down.append(along_ring(near[-1], 1))
    far = [along_ring(down[0], 1), along_ring(up[1], -1)]

    wave = first_wave(corners, chirp, probe)
    wave, saved, windows = first_stage((*near, *up, *far, *down), wave, twiddle)
    wave, intensity = lax.optimization_barrier((wave, intensity))
    intensity_before = lax.ppermute(intensity, "pos", onward)
    for section in range(1, STAGES - 1):
        wave = along_stages(wave, 1)
        wave, saved = forward_stage(section, windows, wave, saved, twiddle)
    wave = along_stages(wave, 1)
    measured = jnp.where(core == 0, intensity[0], intensity_before[1])
    wave, same, other = turn_stage(STAGES - 1, windows, wave, measured, twiddle, chirp)
    for section in reversed(range(1, STAGES - 1)):
        wave = along_stages(wave, -1)
        wave, same, other = backward_stage(
            section, windows, wave, saved, twiddle, chirp, same, other
        )
    wave = along_stages(wave, -1)
    same, other = backward_stage(0, windows, wave, saved, twiddle, chirp, same, other)
    moved_same = across(same, 0, True)
    moved_other = across(other, 1, True)
    other = swap_cores(other)
    pieces = (same, other, moved_same, moved_other)
    return paste_windows(corners, pieces, object_field.shape)


def solution(mesh):
    mapped = jax.shard_map(
        body,
        mesh=mesh,
        in_specs=(
            P("depth", None, "pos", None),
            P("pos", None),
            P(),
            P("pos", None, None),
            P(),
        ),
        out_specs=P("depth", None, "pos", None),
        check_vma=False,
    )
    tables = make_tables()

    def run(object_field, offsets, probe, intensity):
        constants = tuple(jnp.asarray(table) for table in tables)
        return mapped(object_field, offsets, probe, intensity, constants)

    return run
```
